32 devices in a mesh: row: 4 (over y, x), col: 4 (over z), depth: 2 (over core).
Axes of the slice: x: 2, y: 2, z: 4, core: 2. Of those that a mesh axis runs over, the one named last changes fastest.
Arguments:
- left_outer: bfloat16 [4, 8, 2048, 128], P('row', 'depth', 'col'), may hold values from -6 to 6
- left_inner: bfloat16 [4, 8, 2048, 128], P('row', 'depth', 'col'), may hold values from -0.125 to 0.125
- right_outer: bfloat16 [4, 8, 2048, 128], P('col', 'depth', 'row'), may hold values from -6 to 6
- right_inner: bfloat16 [4, 8, 2048, 128], P('col', 'depth', 'row'), may hold values from -0.125 to 0.125
- range_test: bfloat16 [4, 2048, 128], P('col', 'row'), may hold values from -0.125 to 0.125
- corange_test: bfloat16 [4, 2048, 256], P('row', 'col'), may hold values from -0.125 to 0.125
- product_mask: int32 [4, 4, 8], P('row', 'col', 'depth'), may hold values 0 or 1
Outputs:
- range_factor: float32 [4, 4, 2048, 128], P('row', 'col', 'depth')
- corange_factor: float32 [4, 4, 2048, 128], P('row', 'col', 'depth')
The draws below stay inside these ranges and needn't reach their ends.
All inputs are finite; a program needn't handle non-finite values. No bound on the sum of `product_mask` on one device may be relied on, other than what follows from the above.
Results may differ from the reference program's by a relative error of at most 0.0093.
Values may be sent and summed in bfloat16 or wider, within the bound.
A program may use at most 64 MiB of HBM per device.

```python
import jax
import jax.numpy as jnp
from jax import lax

TILE = 2048
RANK = 128
SKETCH = 256
INNER = 8
TILE_ROWS = 4
TILE_COLS = 4


def with_ends(values, key, low, largest):
    spot = [jax.random.randint(jax.random.fold_in(key, axis), (), 0, length) for axis, length in enumerate(values.shape)]
    main_axis = values.shape.index(max(values.shape))
    neighbour = spot[:main_axis] + [(spot[main_axis] + 1) % values.shape[main_axis]] + spot[main_axis + 1:]
    return values.at[tuple(spot)].set(low).at[tuple(neighbour)].set(largest)


def level_of(key, extent, pieces, low, top_value):
    factor_of, own = 1.0, jax.random.fold_in(key, 6)
    for position, shards_of in pieces:
        heights = jnp.exp(jax.random.uniform(jax.random.fold_in(own, position), (shards_of,), jnp.float32, low / len(pieces), top_value / len(pieces)))
        factor_of = factor_of * jnp.repeat(heights, extent[position] // shards_of).reshape([-1 if axis == position else 1 for axis in range(len(extent))])
    return factor_of


def bell_draw(rng, dims, deviation, limit, shards=(), kind=jnp.bfloat16):
    entries = jax.random.normal(rng, dims, jnp.float32) * deviation
    if len(shards) > 0:
        entries = level_of(rng, dims, shards, -0.22, 0.18) * entries
    return jnp.clip(entries, min=-limit, max=limit).astype(kind)


def setup_inputs(seed: int = 0) -> dict:
    arg_keys = jax.random.split(jax.random.key(seed), 8)
    left_outer = bell_draw(arg_keys[0], (TILE_ROWS, INNER, TILE, RANK), 1.0, 6.0, ((0, 4), (1, 2), (2, 4)))
    left_inner = bell_draw(arg_keys[1], (TILE_ROWS, INNER, TILE, RANK), TILE ** -0.5, 0.125, ((0, 4), (1, 2), (2, 4)))
    right_outer = bell_draw(arg_keys[2], (TILE_COLS, INNER, TILE, RANK), 1.0, 6.0, ((0, 4), (1, 2), (2, 4)))
    right_inner = bell_draw(arg_keys[3], (TILE_COLS, INNER, TILE, RANK), TILE ** -0.5, 0.125, ((0, 4), (1, 2), (2, 4)))
    range_test = bell_draw(arg_keys[4], (TILE_COLS, TILE, RANK), TILE ** -0.5, 0.125, ((0, 4), (1, 4)))
    corange_test = bell_draw(arg_keys[5], (TILE_ROWS, TILE, SKETCH), TILE ** -0.5, 0.125, ((0, 4), (1, 4)))
    product_mask = with_ends((jax.random.randint(arg_keys[6], (TILE_ROWS, TILE_COLS, INNER), 0, 2) < 1).astype(jnp.int32), jax.random.fold_in(arg_keys[6], 1), 0, 1)
    return dict(left_outer=left_outer, left_inner=left_inner, right_outer=right_outer, right_inner=right_inner, range_test=range_test, corange_test=corange_test, product_mask=product_mask)


def reference(left_outer, left_inner, right_outer, right_inner, range_test, corange_test, product_mask):
    flt = jnp.float32
    half = jnp.bfloat16
    highest = lax.Precision.HIGHEST
    scale = INNER ** (-0.5)
    probes = []
    for col_tile in range(TILE_COLS):
        probes.append(jnp.einsum('kbr,bs->krs', right_outer[col_tile].astype(flt), range_test[col_tile].astype(flt)).astype(half))
    tests = []
    for row_tile in range(TILE_ROWS):
        tests.append(jnp.einsum('bs,kbr->ksr', corange_test[row_tile].astype(flt), left_outer[row_tile].astype(flt)).astype(half))
    range_rows = []
    corange_rows = []
    for row_tile in range(TILE_ROWS):
        outer_left = left_outer[row_tile].astype(flt)
        inner_left = left_inner[row_tile].astype(flt)
        test_full = corange_test[row_tile].astype(flt)
        range_line = []
        corange_line = []
        for col_tile in range(TILE_COLS):
            cross = jnp.einsum('kbr,kbs->krs', inner_left, right_inner[col_tile].astype(flt)).astype(half)
            weight = (product_mask[row_tile, col_tile].astype(flt) * scale)[:, None, None]
            core_right = (jnp.einsum('krs,kst->krt', cross.astype(flt), probes[col_tile].astype(flt)) * weight).astype(half)
            core_left = (jnp.einsum('kar,krs->kas', tests[row_tile].astype(flt), cross.astype(flt)) * weight).astype(half)
            range_sketch = jnp.einsum('kbr,krs->bs', outer_left, core_right.astype(flt))
            corange_sketch = jnp.einsum('kbs,kas->ba', right_outer[col_tile].astype(flt), core_left.astype(flt))
            core = jnp.dot(test_full.T, range_sketch, precision=highest)
            gram = jnp.dot(core.T, core, precision=highest)
            ridge = 0.05 * jnp.trace(gram) / RANK + 1e-05
            gram = gram + ridge * jnp.eye(RANK, dtype=flt)
            lower = jnp.linalg.cholesky(gram)
            projected = jnp.dot(corange_sketch, core, precision=highest)
            solved = jax.scipy.linalg.cho_solve((lower, True), projected.T).T
            range_line.append(range_sketch)
            corange_line.append(solved * RANK ** 0.5)
        range_rows.append(jnp.stack(range_line))
        corange_rows.append(jnp.stack(corange_line))
    return (jnp.stack(range_rows), jnp.stack(corange_rows))
```

```python
import functools

import jax
import jax.numpy as jnp
from jax import lax
from jax.experimental import pallas as pl
from jax.experimental.pallas import tpu as pltpu
from jax.sharding import PartitionSpec as P

F32 = jnp.float32
BF16 = jnp.bfloat16
HIGHEST = lax.Precision.HIGHEST
MESH = pl.DeviceIdType.MESH
RULER = 32768


def mm(a, b, contract=(1, 0), precision=None):
    dims = (((contract[0],), (contract[1],)), ((), ()))
    return lax.dot_general(a, b, dims, precision=precision, preferred_element_type=F32)


def inverse_schedule(rank):
    low = 1.0 / (rank / 0.05 + 1.0)
    low *= 0.999
    start = 2.0 / (1.0 + low)
    err = 1.0 - low * start
    scales = []
    while err > 1e-3:
        scales.append(2.0 / (2.0 - err * err))
        err = err * err / (2.0 - err * err)
    return start, scales


def kernel(
    sizes,
    lo_h, li_h, ro_h, ri_h, rt_h, ct_h, mask_h,
    out_range, out_corange,
    mask, ruler, lo, ro, ri, rt, ct, lig, rig, rx, tp, tpe, tps, tpo, test, tmid, pps, ppr, probe,
    cx, xs, xr, cps, cpr, crt, clt, zz, rps, rpr, rsend, rout, qps, qpr, qsend, qout,
    load_s, send_s, li_in, ri_in, ext_in, tp_in, te_in, pp_in, pr_in, xr_in, cp_in, cr_in, z_in,
    rp_in, ro_in, qp_in, qo_in,
):
    R, C, D, K = sizes
    KM = K // 2
    KN = K - KM
    KR = K // R
    rank = lo_h.shape[2]
    r, c, d = lax.axis_index("row"), lax.axis_index("col"), lax.axis_index("depth")
    is_end = jnp.logical_or(c == 0, c == C - 1)
    is_mid = jnp.logical_not(is_end)
    across = (r + 1 - 2 * lax.rem(r, 2), lax.rem(r + 2, R), R - 1 - r)
    sent = {}

    def send(branch, src, dst, recv, dev, size, sem=0):
        op = pltpu.make_async_remote_copy(
            src_ref=src, dst_ref=dst, send_sem=send_s.at[sem], recv_sem=recv,
            device_id=dev, device_id_type=MESH,
        )
        op.start()
        sent[branch] = sent.get(branch, 0) + size

    def arrive(ref, recv):
        pltpu.make_async_remote_copy(
            src_ref=ref, dst_ref=ref, send_sem=send_s.at[0], recv_sem=recv,
            device_id=(r, c, d), device_id_type=MESH,
        ).wait_recv()

    def drain(sem, ref):
        pltpu.make_async_remote_copy(
            src_ref=ref, dst_ref=ref, send_sem=send_s.at[sem], recv_sem=load_s.at[0],
            device_id=(r, c, d), device_id_type=MESH,
        ).wait_send()

    def bytes_of(size):
        return ruler.at[pl.ds(0, size // (2 * rank))]

    def load(src, dst, index):
        op = pltpu.make_async_copy(src, dst, load_s.at[index])
        op.start()
        return op

    load_ri = load(ri_h, ri, 0)
    load_ct = load(ct_h, ct, 1)
    for k in range(K):
        load(lo_h.at[k], lo.at[:, pl.ds(k * rank, rank)], 2)
    load_rt = load(rt_h, rt, 3)
    for k in range(K):
        load(ro_h.at[k], ro.at[:, pl.ds(k * rank, rank)], 4)
    load_li = load(li_h, lig.at[c], 5)
    load_mask = load(mask_h, mask, 6)

    bar = pltpu.get_barrier_semaphore()

    @pl.loop(1, R * D)
    def _(o):
        n = lax.rem(r * D + d + o, R * D)
        pl.semaphore_signal(bar, inc=1, device_id=(n // D, c, lax.rem(n, D)), device_id_type=MESH)

    @pl.loop(1, C * D)
    def _(o):
        n = lax.rem(c * D + d + o, C * D)
        pl.semaphore_signal(bar, inc=1, device_id=(r, n // D, lax.rem(n, D)), device_id_type=MESH)

    pl.semaphore_wait(bar, R * D + C * D - 2)

    BLK = lig.shape[2] * rank * 2
    SQ = rank * rank * 2
    sketch = ct_h.shape[1]
    near = 1 + (c // (C - 1)) * (C - 3)
    edge = ((c - 1) // max(C - 3, 1)) * (C - 1)
    other = C - 1 - c
    half = KM * rank

    def send_li(branch, k, owner, dev, src=None):
        send(branch, lig.at[owner, k] if src is None else src, lig.at[owner, k],
             li_in.at[owner, k], dev, BLK)

    def send_ri(branch, k, owner, to, slot):
        send(branch, rig.at[owner, k], rig.at[owner, k], ri_in.at[slot, k], (to, c, d), BLK)

    def relay_ri(branch, k):
        via, to = (0, 1) if k % 2 == 0 else (1, 0)
        arrive(rig.at[across[via], k], ri_in.at[via, k])
        send_ri(branch, k, across[via], across[to], 2)

    def wait_ri(k, skip):
        for slot in range(3):
            if slot != skip:
                arrive(rig.at[across[slot], k], ri_in.at[slot, k])

    def via_of(k):
        return 0 if k % 2 == 0 else 1

    def tall(ref_row, kk, part):
        return rx.at[ref_row, kk, pl.ds(part * rank, rank)]

    def send_x(branch, kk, part, owner, to, slot):
        send(branch, tall(owner, kk, part), tall(owner, kk, part), ext_in.at[part, slot, kk],
             (to, c, d), BLK)

    def relay_x(branch, kk, part):
        via, to = (0, 1) if kk % 2 == 0 else (1, 0)
        arrive(tall(across[via], kk, part), ext_in.at[part, via, kk])
        send_x(branch, kk, part, across[via], across[to], 2)

    def tests():
        load_ct.wait()
        pltpu.make_async_copy(lo, lo, load_s.at[2]).wait()
        tp[...] = mm(ct[...].T, lo[...]).astype(BF16)

    def probes(branch):
        load_rt.wait()
        pltpu.make_async_copy(ro, ro, load_s.at[4]).wait()
        part = mm(rt[...].T, ro[...])
        for n in range(R):
            pps[n] = part[:, n * KR * rank:(n + 1) * KR * rank]
        for slot in range(3):
            send(branch, pps.at[across[slot]], ppr.at[slot], pp_in.at[0],
                 (across[slot], c, d), KR * SQ * 2)

    def probe_sum(branch):
        arrive(ppr, pp_in.at[0])
        total = pps[r]
        for slot in range(3):
            total = total + ppr[slot]
        probe[r] = total.astype(BF16)
        for slot in range(3):
            send(branch, probe.at[r], probe.at[r], pr_in.at[0], (across[slot], c, d), KR * SQ)

    def probe_wait():
        arrive(probe.at[pl.ds(0, 3)], pr_in.at[0])

    scale = (K * D) ** -0.5

    def cross_plain(k):
        total = None
        for b in range(C):
            term = mm(rig[b, k], lig[b, k])
            total = term if total is None else total + term
        return total.astype(BF16)

    def right_of(k, cross):
        weight = mask[0, 0, k].astype(F32) * scale
        lanes = pl.ds(k % KR * rank, rank)
        right = (mm(probe[k // KR, :, lanes], cross) * weight).astype(BF16)
        crt[c, :, pl.ds(k * rank, rank)] = right

    def part_of(n, part):
        return crt.at[n, :, pl.ds(0, KN * rank) if part == 0 else pl.ds(KN * rank, half)]

    def send_crt(branch, owner, part, to):
        send(branch, part_of(owner, part), part_of(owner, part), cr_in.at[owner, part],
             (r, to, d), (KN if part == 0 else KM) * SQ)

    @pl.when(is_mid)
    def _():
        B = "mid"
        for k in range(K):
            send_li(B, k, c, (r, other, d), li_h.at[k])
            if k < KN:
                send_li(B, k, c, (r, edge, d), li_h.at[k])
        load_ri.wait()
        for k in range(KN):
            rig[r, k] = ri[k].T
            for slot in range(2):
                send_ri(B, k, r, across[slot], slot)
        for kk in range(KM):
            rx[r, kk, 0:rank] = ri[KN + kk].T
            for slot in range(2):
                send_x(B, kk, 0, r, across[slot], slot)
        tests()
        probes(B)
        far = C - 1 - edge
        lower = c == 1
        h = jnp.where(lower, 0, 1)
        arrive(lig.at[edge, 0], li_in.at[edge, 0])
        send_li(B, 0, edge, (r, other, d))
        for k in range(KN):
            arrive(lig.at[other, k], li_in.at[other, k])
            send_li(B, k, other, (r, edge, d))
            relay_ri(B, k)
        arrive(tpe, tp_in.at[0])
        both = tpe[...].astype(F32) + tp[...].astype(F32)
        tmid[...] = jnp.where(lower, both[:, 0:half], both[:, half:2 * half])
        tps[...] = jnp.where(lower, both[:, half:2 * half], both[:, 0:half]).astype(BF16)
        send(B, tps, tpo, tp_in.at[1], (r, other, d), sketch * half * 2)
        for k in range(1, KN):
            arrive(lig.at[edge, k], li_in.at[edge, k])
            send_li(B, k, edge, (r, other, d))
        relay_x(B, 0, 0)
        relay_x(B, 1, 0)
        arrive(tall(r, 0, 1), ext_in.at[1, 3, 0])
        for slot in range(2):
            send_x(B, 0, 1, r, across[slot], slot)
        arrive(lig.at[far, 0], li_in.at[far, 0])
        send_li(B, 0, far, (r, edge, d))
        arrive(tpo, tp_in.at[1])
        test[h] = (tmid[...] + tpo[...].astype(F32)).astype(BF16)
        for to in (edge, other):
            send(B, test.at[h], test.at[h], te_in.at[h], (r, to, d), sketch * half * 2)
        arrive(tall(r, 1, 1), ext_in.at[1, 3, 1])
        for slot in range(2):
            send_x(B, 1, 1, r, across[slot], slot)
        probe_sum(B)
        arrive(lig.at[edge, KN], li_in.at[edge, KN])
        send_li(B, KN, edge, (r, other, d))
        for k in range(1, KN):
            arrive(lig.at[far, k], li_in.at[far, k])
            send_li(B, k, far, (r, edge, d))
        for k in range(KN + 1, K):
            arrive(lig.at[edge, k], li_in.at[edge, k])
            send_li(B, k, edge, (r, other, d))
        arrive(test.at[1 - h], te_in.at[1 - h])
        send(B, test.at[1 - h], test.at[1 - h], te_in.at[1 - h], (r, edge, d), sketch * half * 2)
        for kk in range(KM):
            relay_x(B, kk, 1)
        for k in range(KN):
            wait_ri(k, via_of(k))
        probe_wait()
        load_li.wait()
        load_mask.wait()
        for k in range(KN):
            cx[k] = cross_plain(k)
            right_of(k, cx[k])
        for to in (other, edge):
            send_crt(B, c, 0, to)
        for kk in range(KM):
            k = KN + kk
            for part in range(2):
                for slot in range(3):
                    if slot != via_of(kk):
                        arrive(tall(across[slot], kk, part), ext_in.at[part, slot, kk])
            for b in (other, far):
                arrive(lig.at[b, k], li_in.at[b, k])
            total = None
            for b in range(C):
                term = mm(rx[b, kk], lig[b, k])
                total = term if total is None else total + term
            xs[kk] = total[rank:].astype(BF16)
            send(B, xs.at[kk], xr.at[kk], xr_in.at[kk], (r, edge, d), SQ)
            cx[k] = total[:rank].astype(BF16)
        for k in range(KN, K):
            right_of(k, cx[k])
        for to in (edge, other, far):
            send_crt(B, c, 1, to)

    @pl.when(is_end)
    def _():
        B = "end"
        send_li(B, 0, c, (r, near, d), li_h.at[0])
        load_ri.wait()
        for k in range(KN):
            rig[r, k] = ri[k].T
            for slot in range(2):
                send_ri(B, k, r, across[slot], slot)
        tests()
        send(B, tp, tpe, tp_in.at[0], (r, near, d), sketch * K * rank * 2)
        for k in range(1, KN):
            send_li(B, k, c, (r, near, d), li_h.at[k])
        for kk in range(KM):
            rx[r, kk, 0:rank] = ri[KN + kk].T
            send(B, tall(r, kk, 0), tall(r, kk, 1), ext_in.at[1, 3, kk], (r, near, d), BLK)
        for k in range(KN, K):
            send_li(B, k, c, (r, near, d), li_h.at[k])
        probes(B)
        for k in range(KN):
            relay_ri(B, k)
        probe_sum(B)
        for n in (near, C - 1 - near, other):
            for k in range(KN):
                arrive(lig.at[n, k], li_in.at[n, k])
        for k in range(KN):
            wait_ri(k, via_of(k))
        probe_wait()
        load_li.wait()
        load_mask.wait()
        for k in range(KN):
            cx[k] = cross_plain(k)
            right_of(k, cx[k])
        send_crt(B, c, 0, near)
        for h in range(2):
            arrive(test.at[h], te_in.at[h])
        for kk in range(KM):
            arrive(xr.at[kk], xr_in.at[kk])
            cx[KN + kk] = xr[kk]
            right_of(KN + kk, xr[kk])
        for to in (near, C - 1 - near, other):
            send_crt(B, c, 1, to)

    core_part = None
    for k in range(K):
        weight = mask[0, 0, k].astype(F32) * scale
        hk, kk = (0, k) if k < KN else (1, k - KN)
        test_k = test[hk, :, kk * rank:(kk + 1) * rank]
        clt[k] = (mm(cx[k], test_k, (1, 1)) * weight).astype(BF16)
        term = mm(crt[c, :, k * rank:(k + 1) * rank], test_k, (1, 1))
        core_part = term if core_part is None else core_part + term
    cps[...] = core_part
    for o in range(1, D):
        send("cp", cps, cpr.at[d], cp_in.at[0], (r, c, lax.rem(d + o, D)), 0, 3)
    cpr[d] = core_part

    @pl.when(is_mid)
    def _():
        B = "mid"
        arrive(part_of(edge, 0), cr_in.at[edge, 0])
        send_crt(B, edge, 0, other)
        arrive(part_of(other, 0), cr_in.at[other, 0])
        send_crt(B, other, 0, edge)

    arrive(cpr.at[pl.ds(0, D - 1)], cp_in.at[0])
    core = cpr[0]
    for n in range(1, D):
        core = core + cpr[n]

    gram = mm(core, core, (1, 1), HIGHEST)
    eye = (
        lax.broadcasted_iota(jnp.int32, (rank, rank), 0)
        == lax.broadcasted_iota(jnp.int32, (rank, rank), 1)
    ).astype(F32)
    trace = jnp.sum(core * core)
    ridge = 0.05 * trace / rank + 1e-05
    norm = 1.0 / jnp.broadcast_to(trace + ridge, (rank, rank))
    gram = (gram + ridge * eye) * norm
    start, scales = inverse_schedule(rank)
    rest = eye - start * gram
    inv = (scales[0] * start) * (eye + rest)
    rest = (1.0 - scales[0]) * eye + scales[0] * mm(rest, rest, precision=HIGHEST)
    for factor in scales[1:]:
        both = mm(jnp.concatenate([inv, rest], axis=0), rest, precision=HIGHEST)
        inv = factor * (inv + both[:rank])
        rest = (1.0 - factor) * eye + factor * both[rank:]
    for _ in range(1):
        inv = inv + mm(inv, eye - mm(gram, inv, precision=HIGHEST), precision=HIGHEST)
    weights = (mm(inv, core, precision=HIGHEST) * (norm[:, 0:1] * rank**0.5)).astype(BF16)

    rows = KN * rank

    def zpart(n, part):
        return zz.at[n, pl.ds(0, rows) if part == 0 else pl.ds(rows, half)]

    for part in range(2):
        for k in range(KN) if part == 0 else range(KN, K):
            zz[r, pl.ds(k * rank, rank)] = mm(clt[k], weights, (1, 1)).astype(BF16)
        for slot in range(2):
            send("all", zpart(r, part), zpart(r, part), z_in.at[slot, part], (across[slot], c, d),
                 (KN if part == 0 else KM) * SQ)

    @pl.when(is_mid)
    def _():
        B = "mid"
        far = C - 1 - edge
        arrive(part_of(far, 0), cr_in.at[far, 0])
        send_crt(B, far, 0, edge)

    def relay_z(part):
        via, to = (0, 1) if part == 0 else (1, 0)
        arrive(zpart(across[via], part), z_in.at[via, part])
        send("all", zpart(across[via], part), zpart(across[via], part), z_in.at[2, part],
             (across[to], c, d), (KN if part == 0 else KM) * SQ)

    part_l = lo_h.shape[1] // D
    place = c * D + d
    owner, slot_l = place // C, lax.rem(place, C)

    def range_mm(j, index):
        total = mm(lo[...], crt[j], (1, 1))
        for n in range(D):
            rps[n, index] = total[n * part_l:(n + 1) * part_l]
        for e in range(1, D):
            n = lax.rem(d + e, D)
            send("rp", rps.at[n, index], rpr.at[index, d], rp_in.at[index], (r, c, n), 0, 4)

    def range_out(j, index, first):
        total = rps[d, index]
        arrive(rpr.at[index, pl.ds(0, D - 1)], rp_in.at[index])
        for e in range(1, D):
            total = total + rpr[index, lax.rem(d + e, D)]
        rsend[index] = total.astype(BF16)
        if first:
            @pl.when(owner != d)
            def _():
                send("ro", rsend.at[index], rout.at[slot_l], ro_in.at[slot_l], (r, j, owner), part_l * rank * 2, 1)
        else:
            send("all", rsend.at[index], rout.at[slot_l], ro_in.at[slot_l], (r, j, owner), part_l * rank * 2)

    range_mm(c, 0)
    relay_z(0)
    relay_z(1)

    for o in range(1, C):
        n = lax.rem(c + o, C)
        arrive(part_of(n, 1), cr_in.at[n, 1])

    @pl.when(is_end)
    def _():
        for o in range(1, C):
            n = lax.rem(c + o, C)
            arrive(part_of(n, 0), cr_in.at[n, 0])

    for o in range(1, C):
        range_mm(lax.rem(c + o, C), o)
    for o in range(C):
        range_out(lax.rem(c + o, C), o, o == 0)

    part_r = ro_h.shape[1] // D
    place_q = r * D + d
    owner_q, slot_q = place_q // R, lax.rem(place_q, R)

    def corange_mm(i, index):
        total = mm(ro[...], zz[i])
        for n in range(D):
            qps[n, index] = total[n * part_r:(n + 1) * part_r]
        for e in range(1, D):
            n = lax.rem(d + e, D)
            send("qp", qps.at[n, index], qpr.at[index, d], qp_in.at[index], (r, c, n), 0, 5)

    def corange_out(i, index, first):
        total = qps[d, index]
        arrive(qpr.at[index, pl.ds(0, D - 1)], qp_in.at[index])
        for e in range(1, D):
            total = total + qpr[index, lax.rem(d + e, D)]
        qsend[index] = total.astype(BF16)
        if first:
            @pl.when(owner_q != d)
            def _():
                send("qo", qsend.at[index], qout.at[slot_q], qo_in.at[slot_q], (i, c, owner_q), part_r * rank * 2, 2)
        else:
            send("all", qsend.at[index], qout.at[slot_q], qo_in.at[slot_q], (i, c, owner_q), part_r * rank * 2)

    corange_mm(r, 0)
    arrive(zpart(across[0], 1), z_in.at[0, 1])
    corange_mm(across[0], 1)
    arrive(zpart(across[1], 0), z_in.at[1, 0])
    corange_mm(across[1], 2)
    for part in range(2):
        arrive(zpart(across[2], part), z_in.at[2, part])
    corange_mm(across[2], 3)
    corange_out(r, 0, True)
    for slot in range(3):
        corange_out(across[slot], slot + 1, False)

    @pl.when(owner == d)
    def _():
        rout[slot_l] = rsend[0]

    @pl.when(owner_q == d)
    def _():
        qout[slot_q] = qsend[0]

    for q in range(C):
        src = d * C + q
        mine = jnp.logical_and(src // D == c, lax.rem(src, D) == d)

        @pl.when(jnp.logical_not(mine))
        def _(q=q):
            arrive(rout.at[q], ro_in.at[q])

        out_range[q * part_l:(q + 1) * part_l, :] = rout[q]
    for q in range(R):
        src = d * R + q
        mine = jnp.logical_and(src // D == r, lax.rem(src, D) == d)

        @pl.when(jnp.logical_not(mine))
        def _(q=q):
            arrive(qout.at[q], qo_in.at[q])

        out_corange[q * part_r:(q + 1) * part_r, :] = qout[q]

    drain(3, cpr.at[pl.ds(0, D - 1)])
    drain(4, rpr.at[:, pl.ds(0, D - 1)])
    drain(5, qpr.at[:, pl.ds(0, D - 1)])
    for branch, cond in (("mid", is_mid), ("end", is_end)):
        @pl.when(cond)
        def _(branch=branch):
            drain(0, bytes_of(sent["all"] + sent[branch]))
    for branch, cond, sem in (("ro", owner != d, 1), ("qo", owner_q != d, 2)):
        @pl.when(cond)
        def _(branch=branch, sem=sem):
            drain(sem, bytes_of(sent[branch]))


def body(sizes, left_outer, left_inner, right_outer, right_inner, range_test, corange_test, product_mask):
    R, C, D = sizes
    K, BL, rank = left_outer.shape[1:]
    BR = right_outer.shape[2]
    sketch = corange_test.shape[2]
    assert R == 4 and C == 4 and K % R == 0 and BL == BR and BL % D == 0 and D > 1
    KM = K // 2
    KN = K - KM
    KR = K // R
    dma = pltpu.SemaphoreType.DMA
    vmem = pltpu.VMEM
    scratch = [
        pltpu.SMEM((1, 1, K), jnp.int32),
        vmem((RULER, rank), BF16),
        vmem((BL, K * rank), BF16),
        vmem((BR, K * rank), BF16),
        vmem((K, BR, rank), BF16),
        vmem((BR, rank), BF16),
        vmem((BL, sketch), BF16),
        vmem((C, K, BL, rank), BF16),
        vmem((R, KN, rank, BR), BF16),
        vmem((R, KM, 2 * rank, BR), BF16),
        vmem((sketch, K * rank), BF16),
        vmem((sketch, K * rank), BF16),
        vmem((sketch, KM * rank), BF16),
        vmem((sketch, KM * rank), BF16),
        vmem((2, sketch, KM * rank), BF16),
        vmem((sketch, KM * rank), F32),
        vmem((R, rank, KR * rank), F32),
        vmem((R - 1, rank, KR * rank), F32),
        vmem((R, rank, KR * rank), BF16),
        vmem((K, rank, rank), BF16),
        vmem((KM, rank, rank), BF16),
        vmem((KM, rank, rank), BF16),
        vmem((rank, sketch), F32),
        vmem((D, rank, sketch), F32),
        vmem((C, rank, K * rank), BF16),
        vmem((K, rank, sketch), BF16),
        vmem((R, K * rank, rank), BF16),
        vmem((D, C, BL // D, rank), F32),
        vmem((C, D, BL // D, rank), F32),
        vmem((C, BL // D, rank), BF16),
        vmem((C, BL // D, rank), BF16),
        vmem((D, R, BR // D, rank), F32),
        vmem((R, D, BR // D, rank), F32),
        vmem((R, BR // D, rank), BF16),
        vmem((R, BR // D, rank), BF16),
        dma((7,)), dma((6,)),
        dma((C, K)), dma((3, KN)), dma((2, 4, KM)), dma((2,)), dma((2,)), dma((1,)), dma((1,)), dma((KM,)),
        dma((1,)), dma((C, 2)), dma((3, 2)), dma((C,)), dma((C,)), dma((R,)), dma((R,)),
    ]
    whole = pl.BlockSpec(memory_space=pltpu.VMEM)
    out = jax.ShapeDtypeStruct((BL * C // D, rank), BF16)
    range_rows, corange_rows = pl.pallas_call(
        functools.partial(kernel, (R, C, D, K)),
        out_shape=(out, out),
        in_specs=[pl.BlockSpec(memory_space=pltpu.HBM)] * 7,
        out_specs=(whole, whole),
        scratch_shapes=scratch,
        compiler_params=pltpu.CompilerParams(
            collective_id=0, has_side_effects=True, vmem_limit_bytes=36 * 1024 * 1024
        ),
    )(*[
        pltpu.with_memory_space_constraint(x, pltpu.HBM)
        for x in (left_outer[0], left_inner[0], right_outer[0], right_inner[0],
                  range_test[0], corange_test[0], product_mask)
    ])
    return range_rows[None, None].astype(F32), corange_rows[None, None].astype(F32)


def solution(mesh):
    sizes = tuple(mesh.shape[name] for name in ("row", "col", "depth"))
    return jax.shard_map(
        functools.partial(body, sizes),
        mesh=mesh,
        in_specs=(
            P("row", "depth", "col", None),
            P("row", "depth", "col", None),
            P("col", "depth", "row", None),
            P("col", "depth", "row", None),
            P("col", "row", None),
            P("row", "col", None),
            P("row", "col", "depth"),
        ),
        out_specs=(P("row", "col", "depth", None), P("row", "col", "depth", None)),
        check_vma=False,
    )
```

```python
import functools

import jax
import jax.numpy as jnp
from jax import lax
from jax.experimental import pallas as pl
from jax.experimental.pallas import tpu as pltpu
from jax.sharding import PartitionSpec as P

F32 = jnp.float32
BF16 = jnp.bfloat16
HIGHEST = lax.Precision.HIGHEST
MESH = pl.DeviceIdType.MESH
RULER = 32768


def mm(a, b, contract=(1, 0), precision=None):
    dims = (((contract[0],), (contract[1],)), ((), ()))
    return lax.dot_general(a, b, dims, precision=precision, preferred_element_type=F32)


def mm_split(a, b):
    a_up, b_up = a.astype(BF16), b.astype(BF16)
    a_low, b_low = (a - a_up.astype(F32)).astype(BF16), (b - b_up.astype(F32)).astype(BF16)
    return mm(jnp.concatenate([a_up, a_up, a_low], axis=1), jnp.concatenate([b_up, b_low, b_up], axis=0))


def inverse_schedule(rank):
    low = 1.0 / (rank / 0.05 + 1.0)
    low *= 0.999
    start = 2.0 / (1.0 + low)
    err = 1.0 - low * start
    scales = []
    while err > 1e-3:
        scales.append(2.0 / (2.0 - err * err))
        err = err * err / (2.0 - err * err)
    return start, scales


def kernel(
    sizes,
    lo_h, li_h, ro_h, ri_h, rt_h, ct_h, mask_h,
    out_range, out_corange,
    mask, ruler, lo, ro, ri, rt, ct, lig, rig, rx, qx, ex, tp, tpe, tps, tpo, test, tmid, pps, ppr, probe,
    cx, xs, xr, cps, cpr, crt, clt, zz, rps, rpr, rsend, rout, qps, qpr, qsend, qout,
    load_s, send_s, li_in, ri_in, ext_in, tp_in, te_in, pp_in, pr_in, xr_in, cp_in, cr_in, z_in,
    rp_in, ro_in, qp_in, qo_in,
):
    R, C, D, K = sizes
    KM = K // 2
    KN = K - KM
    KQ = KN // 2
    KR = K // R
    rank = lo_h.shape[2]
    r, c, d = lax.axis_index("row"), lax.axis_index("col"), lax.axis_index("depth")
    is_end = jnp.logical_or(c == 0, c == C - 1)
    is_mid = jnp.logical_not(is_end)
    across = (r + 1 - 2 * lax.rem(r, 2), lax.rem(r + 2, R), R - 1 - r)
    sent = {}

    def send(branch, src, dst, recv, dev, size, sem=0):
        op = pltpu.make_async_remote_copy(
            src_ref=src, dst_ref=dst, send_sem=send_s.at[sem], recv_sem=recv,
            device_id=dev, device_id_type=MESH,
        )
        op.start()
        sent[branch] = sent.get(branch, 0) + size

    def arrive(ref, recv):
        pltpu.make_async_remote_copy(
            src_ref=ref, dst_ref=ref, send_sem=send_s.at[0], recv_sem=recv,
            device_id=(r, c, d), device_id_type=MESH,
        ).wait_recv()

    def drain(sem, ref):
        pltpu.make_async_remote_copy(
            src_ref=ref, dst_ref=ref, send_sem=send_s.at[sem], recv_sem=load_s.at[0],
            device_id=(r, c, d), device_id_type=MESH,
        ).wait_send()

    def bytes_of(size):
        return ruler.at[pl.ds(0, size // (2 * rank))]

    def load(src, dst, index):
        op = pltpu.make_async_copy(src, dst, load_s.at[index])
        op.start()
        return op

    load_ri = load(ri_h, ri, 0)
    load_ct = load(ct_h, ct, 1)
    for k in range(K):
        load(lo_h.at[k], lo.at[:, pl.ds(k * rank, rank)], 2)
    load_rt = load(rt_h, rt, 3)
    for k in range(K):
        load(ro_h.at[k], ro.at[:, pl.ds(k * rank, rank)], 4)
    load_li = load(li_h, lig.at[c], 5)
    load_mask = load(mask_h, mask, 6)

    bar = pltpu.get_barrier_semaphore()

    @pl.loop(1, R * D)
    def _(o):
        n = lax.rem(r * D + d + o, R * D)
        pl.semaphore_signal(bar, inc=1, device_id=(n // D, c, lax.rem(n, D)), device_id_type=MESH)

    @pl.loop(1, C * D)
    def _(o):
        n = lax.rem(c * D + d + o, C * D)
        pl.semaphore_signal(bar, inc=1, device_id=(r, n // D, lax.rem(n, D)), device_id_type=MESH)

    pl.semaphore_wait(bar, R * D + C * D - 2)

    BLK = lig.shape[2] * rank * 2
    SQ = rank * rank * 2
    sketch = ct_h.shape[1]
    near = 1 + (c // (C - 1)) * (C - 3)
    edge = ((c - 1) // max(C - 3, 1)) * (C - 1)
    other = C - 1 - c
    half = KM * rank

    def send_li(branch, k, owner, dev, src=None):
        send(branch, lig.at[owner, k] if src is None else src, lig.at[owner, k],
             li_in.at[owner, k], dev, BLK)

    def send_ri(branch, k, owner, to, slot):
        send(branch, rig.at[owner, k - KQ], rig.at[owner, k - KQ], ri_in.at[slot, k - KQ], (to, c, d), BLK)

    def relay_ri(branch, k):
        via, to = (0, 1) if k % 2 == 0 else (1, 0)
        arrive(rig.at[across[via], k - KQ], ri_in.at[via, k - KQ])
        send_ri(branch, k, across[via], across[to], 2)

    def wait_ri(k, skip):
        for slot in range(3):
            if slot != skip:
                arrive(rig.at[across[slot], k - KQ], ri_in.at[slot, k - KQ])

    def via_of(k):
        return 0 if k % 2 == 0 else 1

    def tall(ref_row, kk, part):
        return rx.at[ref_row, kk, pl.ds(part * rank, rank)]

    def send_x(branch, kk, part, owner, to, slot):
        send(branch, tall(owner, kk, part), tall(owner, kk, part), ext_in.at[part, slot, kk],
             (to, c, d), BLK)

    def relay_x(branch, kk, part):
        via, to = (0, 1) if (kk + part) % 2 == 0 else (1, 0)
        arrive(tall(across[via], kk, part), ext_in.at[part, via, kk])
        send_x(branch, kk, part, across[via], across[to], 2)

    def wait_x(kk, part):
        for slot in range(3):
            if slot != (kk + part) % 2:
                arrive(tall(across[slot], kk, part), ext_in.at[part, slot, kk])

    def cross_tall(kk, k, to):
        total = None
        for b in range(C):
            term = mm(rx[b, kk], lig[b, k])
            total = term if total is None else total + term
        xs[kk] = total[rank:].astype(BF16)
        send("mid" if k >= KN else "end", xs.at[kk], xr.at[kk], xr_in.at[kk], (r, to, d), SQ)
        cx[k] = total[:rank].astype(BF16)

    def tests():
        load_ct.wait()
        pltpu.make_async_copy(lo, lo, load_s.at[2]).wait()
        tp[...] = mm(ct[...].T, lo[...]).astype(BF16)

    def probes(branch):
        load_rt.wait()
        pltpu.make_async_copy(ro, ro, load_s.at[4]).wait()
        part = mm(rt[...].T, ro[...])
        for n in range(R):
            pps[n] = part[:, n * KR * rank:(n + 1) * KR * rank]
        for slot in range(3):
            send(branch, pps.at[across[slot]], ppr.at[slot], pp_in.at[0],
                 (across[slot], c, d), KR * SQ * 2)

    def probe_sum(branch):
        arrive(ppr, pp_in.at[0])
        total = pps[r]
        for slot in range(3):
            total = total + ppr[slot]
        probe[r] = total.astype(BF16)
        for slot in range(3):
            send(branch, probe.at[r], probe.at[r], pr_in.at[0], (across[slot], c, d), KR * SQ)

    def probe_wait():
        arrive(probe.at[pl.ds(0, 3)], pr_in.at[0])

    scale = (K * D) ** -0.5

    def cross_plain(k):
        total = None
        for b in range(C):
            term = mm(rig[b, k - KQ], lig[b, k])
            total = term if total is None else total + term
        return total.astype(BF16)

    def right_of(k, cross):
        weight = mask[0, 0, k].astype(F32) * scale
        lanes = pl.ds(k % KR * rank, rank)
        right = (mm(probe[k // KR, :, lanes], cross) * weight).astype(BF16)
        crt[c, :, pl.ds(k * rank, rank)] = right

    def part_of(n, part):
        return crt.at[n, :, pl.ds(0, KN * rank) if part == 0 else pl.ds(KN * rank, half)]

    def send_crt(branch, owner, part, to):
        send(branch, part_of(owner, part), part_of(owner, part), cr_in.at[owner, part],
             (r, to, d), (KN if part == 0 else KM) * SQ)

    @pl.when(is_mid)
    def _():
        B = "mid"
        for k in range(K):
            send_li(B, k, c, (r, other, d), li_h.at[k])
            if k < KN:
                send_li(B, k, c, (r, edge, d), li_h.at[k])
        load_ri.wait()
        for k in range(KQ):
            qx[k] = ri[k].T
            send(B, qx.at[k], tall(r, k, 1), ext_in.at[1, 3, k], (r, edge, d), BLK)
        for k in range(KQ, KN):
            rig[r, k - KQ] = ri[k].T
            for slot in range(2):
                send_ri(B, k, r, across[slot], slot)
        for kk in range(KM):
            rx[r, kk, 0:rank] = ri[KN + kk].T
            for slot in range(2):
                send_x(B, kk, 0, r, across[slot], slot)
        tests()
        probes(B)
        far = C - 1 - edge
        lower = c == 1
        h = jnp.where(lower, 0, 1)
        arrive(lig.at[edge, 0], li_in.at[edge, 0])
        send_li(B, 0, edge, (r, other, d))
        for k in range(KN):
            arrive(lig.at[other, k], li_in.at[other, k])
            send_li(B, k, other, (r, edge, d))
            if k >= KQ:
                relay_ri(B, k)
        arrive(tpe, tp_in.at[0])
        both = tpe[...].astype(F32) + tp[...].astype(F32)
        tmid[...] = jnp.where(lower, both[:, 0:half], both[:, half:2 * half])
        tps[...] = jnp.where(lower, both[:, half:2 * half], both[:, 0:half]).astype(BF16)
        send(B, tps, tpo, tp_in.at[1], (r, other, d), sketch * half * 2)
        for k in range(1, KN):
            arrive(lig.at[edge, k], li_in.at[edge, k])
            send_li(B, k, edge, (r, other, d))
        probe_sum(B)
        relay_x(B, 0, 0)
        relay_x(B, 1, 0)
        arrive(tall(r, 0, 1), ext_in.at[1, 3, 0])
        for slot in range(2):
            send_x(B, 0, 1, r, across[slot], slot)
        arrive(lig.at[far, 0], li_in.at[far, 0])
        send_li(B, 0, far, (r, edge, d))
        arrive(tpo, tp_in.at[1])
        test[h] = (tmid[...] + tpo[...].astype(F32)).astype(BF16)
        for to in (edge, other):
            send(B, test.at[h], test.at[h], te_in.at[h], (r, to, d), sketch * half * 2)
        arrive(tall(r, 1, 1), ext_in.at[1, 3, 1])
        for slot in range(2):
            send_x(B, 1, 1, r, across[slot], slot)
        arrive(lig.at[edge, KN], li_in.at[edge, KN])
        send_li(B, KN, edge, (r, other, d))
        for k in range(1, KN):
            arrive(lig.at[far, k], li_in.at[far, k])
            send_li(B, k, far, (r, edge, d))
        for k in range(KN + 1, K):
            arrive(lig.at[edge, k], li_in.at[edge, k])
            send_li(B, k, edge, (r, other, d))
        arrive(test.at[1 - h], te_in.at[1 - h])
        send(B, test.at[1 - h], test.at[1 - h], te_in.at[1 - h], (r, edge, d), sketch * half * 2)
        for kk in range(KM):
            relay_x(B, kk, 1)
        for k in range(KQ, KN):
            wait_ri(k, via_of(k))
        load_li.wait()
        load_mask.wait()
        for k in range(KQ, KN):
            cx[k] = cross_plain(k)
        probe_wait()
        for k in range(KQ, KN):
            right_of(k, cx[k])
        for k in range(KQ):
            arrive(xr.at[k], xr_in.at[k])
            cx[k] = xr[k]
            right_of(k, cx[k])
        send_crt(B, c, 0, other)
        send_crt(B, c, 0, edge)
        for kk in range(KM):
            for part in range(2):
                wait_x(kk, part)
            for b in (other, far):
                arrive(lig.at[b, KN + kk], li_in.at[b, KN + kk])
            cross_tall(kk, KN + kk, edge)
        for k in range(KN, K):
            right_of(k, cx[k])
        send_crt(B, c, 1, other)

    @pl.when(is_end)
    def _():
        B = "end"
        send_li(B, 0, c, (r, near, d), li_h.at[0])
        load_ri.wait()
        for k in range(KQ):
            rx[r, k, 0:rank] = ri[k].T
            for slot in range(2):
                send_x(B, k, 0, r, across[slot], slot)
        for k in range(KQ, KN):
            rig[r, k - KQ] = ri[k].T
            for slot in range(2):
                send_ri(B, k, r, across[slot], slot)
        tests()
        send(B, tp, tpe, tp_in.at[0], (r, near, d), sketch * K * rank * 2)
        for k in range(1, KN):
            send_li(B, k, c, (r, near, d), li_h.at[k])
        for kk in range(KM):
            ex[kk] = ri[KN + kk].T
            send(B, ex.at[kk], tall(r, kk, 1), ext_in.at[1, 3, kk], (r, near, d), BLK)
        for k in range(KN, K):
            send_li(B, k, c, (r, near, d), li_h.at[k])
        probes(B)
        for k in range(KQ):
            relay_x(B, k, 0)
        for k in range(KQ, KN):
            relay_ri(B, k)
        for k in range(KQ):
            arrive(tall(r, k, 1), ext_in.at[1, 3, k])
            for slot in range(2):
                send_x(B, k, 1, r, across[slot], slot)
        probe_sum(B)
        for k in range(KQ):
            relay_x(B, k, 1)
        load_li.wait()
        load_mask.wait()
        probe_wait()
        for k in range(KQ):
            for part in range(2):
                wait_x(k, part)
            for n in (near, C - 1 - near, other):
                arrive(lig.at[n, k], li_in.at[n, k])
            cross_tall(k, k, near)
            right_of(k, cx[k])
        for k in range(KQ, KN):
            wait_ri(k, via_of(k))
            for n in (near, C - 1 - near, other):
                arrive(lig.at[n, k], li_in.at[n, k])
            cx[k] = cross_plain(k)
            right_of(k, cx[k])
        send_crt(B, c, 0, near)
        for h in range(2):
            arrive(test.at[h], te_in.at[h])
        for kk in range(KM):
            arrive(xr.at[kk], xr_in.at[kk])
            cx[KN + kk] = xr[kk]
            right_of(KN + kk, xr[kk])
        for to in (other, C - 1 - near, near):
            send_crt(B, c, 1, to)

    core_part = None
    for k in range(K):
        weight = mask[0, 0, k].astype(F32) * scale
        hk, kk = (0, k) if k < KN else (1, k - KN)
        test_k = test[hk, :, kk * rank:(kk + 1) * rank]
        clt[k] = (mm(cx[k], test_k, (1, 1)) * weight).astype(BF16)
        term = mm(crt[c, :, k * rank:(k + 1) * rank], test_k, (1, 1))
        core_part = term if core_part is None else core_part + term
    cps[...] = core_part
    for o in range(1, D):
        send("cp", cps, cpr.at[d], cp_in.at[0], (r, c, lax.rem(d + o, D)), 0, 3)
    cpr[d] = core_part

    @pl.when(is_mid)
    def _():
        B = "mid"
        arrive(part_of(edge, 0), cr_in.at[edge, 0])
        send_crt(B, edge, 0, other)

    arrive(cpr.at[pl.ds(0, D - 1)], cp_in.at[0])
    core = cpr[0]
    for n in range(1, D):
        core = core + cpr[n]

    def relay_other(part):
        @pl.when(is_mid)
        def _():
            if part == 0:
                send_crt("mid", c, 1, edge)
            arrive(part_of(other, part), cr_in.at[other, part])
            send_crt("mid", other, part, edge)

    relay_other(0)
    gram = mm(core, core, (1, 1), HIGHEST)
    eye = (
        lax.broadcasted_iota(jnp.int32, (rank, rank), 0)
        == lax.broadcasted_iota(jnp.int32, (rank, rank), 1)
    ).astype(F32)
    trace = jnp.sum(core * core)
    ridge = 0.05 * trace / rank + 1e-05
    norm = 1.0 / jnp.broadcast_to(trace + ridge, (rank, rank))
    gram = (gram + ridge * eye) * norm
    start, scales = inverse_schedule(rank)
    rest = eye - start * gram
    inv = (scales[0] * start) * (eye + rest)
    rest = (1.0 - scales[0]) * eye + scales[0] * mm_split(rest, rest)
    for step, factor in enumerate(scales[1:]):
        if step == 5:
            relay_other(1)
        both = mm_split(jnp.concatenate([inv, rest], axis=0), rest)
        inv = factor * (inv + both[:rank])
        rest = (1.0 - factor) * eye + factor * both[rank:]
    solved = mm_split(inv, core)
    solved = solved + mm_split(inv, core - mm(gram, solved, precision=HIGHEST))
    weights = (solved * (norm[:, 0:1] * rank**0.5)).astype(BF16)

    rows = KN * rank

    def zpart(n, part):
        return zz.at[n, pl.ds(0, rows) if part == 0 else pl.ds(rows, half)]

    for part in range(2):
        for k in range(KN) if part == 0 else range(KN, K):
            zz[r, pl.ds(k * rank, rank)] = mm(clt[k], weights, (1, 1)).astype(BF16)
        for slot in range(2):
            send("all", zpart(r, part), zpart(r, part), z_in.at[slot, part], (across[slot], c, d),
                 (KN if part == 0 else KM) * SQ)

    @pl.when(is_mid)
    def _():
        B = "mid"
        far = C - 1 - edge
        arrive(part_of(far, 0), cr_in.at[far, 0])
        send_crt(B, far, 0, edge)

    def relay_z(part, branch):
        via, to = (0, 1) if part == 0 else (1, 0)
        arrive(zpart(across[via], part), z_in.at[via, part])
        send(branch, zpart(across[via], part), zpart(across[via], part), z_in.at[2, part],
             (across[to], c, d), (KN if part == 0 else KM) * SQ)

    part_l = lo_h.shape[1] // D
    place = c * D + d
    owner, slot_l = place // C, lax.rem(place, C)

    def halves(left, right, contract, parts, got, sem, in_s, index):
        size = left.shape[0] // D
        if D == 2:
            for n in (1 - d, d):
                rows = left[pl.ds(pl.multiple_of(n * size, size), size), :]
                parts[n, index] = mm(rows, right, contract)
                if n is not d:
                    send(sem[0], parts.at[n, index], got.at[index, d], in_s.at[index], (r, c, n), 0, sem[1])
        else:
            total = mm(left[...], right, contract)
            for n in range(D):
                parts[n, index] = total[n * size:(n + 1) * size]
            for e in range(1, D):
                n = lax.rem(d + e, D)
                send(sem[0], parts.at[n, index], got.at[index, d], in_s.at[index], (r, c, n), 0, sem[1])

    def range_mm(j, index):
        halves(lo, crt[j], (1, 1), rps, rpr, ("rp", 4), rp_in, index)

    def range_out(j, index, first):
        total = rps[d, index]
        arrive(rpr.at[index, pl.ds(0, D - 1)], rp_in.at[index])
        for e in range(1, D):
            total = total + rpr[index, lax.rem(d + e, D)]
        rsend[index] = total.astype(BF16)
        if first:
            @pl.when(owner != d)
            def _():
                send("ro", rsend.at[index], rout.at[slot_l], ro_in.at[slot_l], (r, j, owner), part_l * rank * 2, 1)
        else:
            send("all", rsend.at[index], rout.at[slot_l], ro_in.at[slot_l], (r, j, owner), part_l * rank * 2)

    range_mm(c, 0)

    @pl.when(is_mid)
    def _():
        relay_z(0, "mid")
        relay_z(1, "mid")
        for n in (C - 1 - edge, edge):
            arrive(part_of(n, 1), cr_in.at[n, 1])

    @pl.when(is_end)
    def _():
        for n in (near, C - 1 - near, other):
            for part in range(2):
                arrive(part_of(n, part), cr_in.at[n, part])

    for o in range(1, C):
        range_mm(lax.rem(c + o, C), o)

    @pl.when(is_end)
    def _():
        relay_z(0, "end")
        relay_z(1, "end")

    for o in range(C):
        range_out(lax.rem(c + o, C), o, o == 0)

    part_r = ro_h.shape[1] // D
    place_q = r * D + d
    owner_q, slot_q = place_q // R, lax.rem(place_q, R)

    def corange_mm(i, index):
        halves(ro, zz[i], (1, 0), qps, qpr, ("qp", 5), qp_in, index)

    def corange_out(i, index, first):
        total = qps[d, index]
        arrive(qpr.at[index, pl.ds(0, D - 1)], qp_in.at[index])
        for e in range(1, D):
            total = total + qpr[index, lax.rem(d + e, D)]
        qsend[index] = total.astype(BF16)
        if first:
            @pl.when(owner_q != d)
            def _():
                send("qo", qsend.at[index], qout.at[slot_q], qo_in.at[slot_q], (i, c, owner_q), part_r * rank * 2, 2)
        else:
            send("all", qsend.at[index], qout.at[slot_q], qo_in.at[slot_q], (i, c, owner_q), part_r * rank * 2)

    corange_mm(r, 0)
    arrive(zpart(across[0], 1), z_in.at[0, 1])
    corange_mm(across[0], 1)
    arrive(zpart(across[1], 0), z_in.at[1, 0])
    corange_mm(across[1], 2)
    for part in range(2):
        arrive(zpart(across[2], part), z_in.at[2, part])
    corange_mm(across[2], 3)
    corange_out(r, 0, True)
    for slot in range(3):
        corange_out(across[slot], slot + 1, False)

    @pl.when(owner == d)
    def _():
        rout[slot_l] = rsend[0]

    @pl.when(owner_q == d)
    def _():
        qout[slot_q] = qsend[0]

    for q in range(C):
        src = d * C + q
        mine = jnp.logical_and(src // D == c, lax.rem(src, D) == d)

        @pl.when(jnp.logical_not(mine))
        def _(q=q):
            arrive(rout.at[q], ro_in.at[q])

        out_range[q * part_l:(q + 1) * part_l, :] = rout[q]
    for q in range(R):
        src = d * R + q
        mine = jnp.logical_and(src // D == r, lax.rem(src, D) == d)

        @pl.when(jnp.logical_not(mine))
        def _(q=q):
            arrive(qout.at[q], qo_in.at[q])

        out_corange[q * part_r:(q + 1) * part_r, :] = qout[q]

    drain(3, cpr.at[pl.ds(0, D - 1)])
    drain(4, rpr.at[:, pl.ds(0, D - 1)])
    drain(5, qpr.at[:, pl.ds(0, D - 1)])
    for branch, cond in (("mid", is_mid), ("end", is_end)):
        @pl.when(cond)
        def _(branch=branch):
            drain(0, bytes_of(sent["all"] + sent[branch]))
    for branch, cond, sem in (("ro", owner != d, 1), ("qo", owner_q != d, 2)):
        @pl.when(cond)
        def _(branch=branch, sem=sem):
            drain(sem, bytes_of(sent[branch]))


def body(sizes, left_outer, left_inner, right_outer, right_inner, range_test, corange_test, product_mask):
    R, C, D = sizes
    K, BL, rank = left_outer.shape[1:]
    BR = right_outer.shape[2]
    sketch = corange_test.shape[2]
    assert R == 4 and C == 4 and K % R == 0 and BL == BR and BL % D == 0 and D > 1
    KM = K // 2
    KN = K - KM
    KQ = KN // 2
    KR = K // R
    dma = pltpu.SemaphoreType.DMA
    vmem = pltpu.VMEM
    scratch = [
        pltpu.SMEM((1, 1, K), jnp.int32),
        vmem((RULER, rank), BF16),
        vmem((BL, K * rank), BF16),
        vmem((BR, K * rank), BF16),
        vmem((K, BR, rank), BF16),
        vmem((BR, rank), BF16),
        vmem((BL, sketch), BF16),
        vmem((C, K, BL, rank), BF16),
        vmem((R, KN - KQ, rank, BR), BF16),
        vmem((R, KM, 2 * rank, BR), BF16),
        vmem((KQ, rank, BR), BF16),
        vmem((KM, rank, BR), BF16),
        vmem((sketch, K * rank), BF16),
        vmem((sketch, K * rank), BF16),
        vmem((sketch, KM * rank), BF16),
        vmem((sketch, KM * rank), BF16),
        vmem((2, sketch, KM * rank), BF16),
        vmem((sketch, KM * rank), F32),
        vmem((R, rank, KR * rank), F32),
        vmem((R - 1, rank, KR * rank), F32),
        vmem((R, rank, KR * rank), BF16),
        vmem((K, rank, rank), BF16),
        vmem((KM, rank, rank), BF16),
        vmem((KM, rank, rank), BF16),
        vmem((rank, sketch), F32),
        vmem((D, rank, sketch), F32),
        vmem((C, rank, K * rank), BF16),
        vmem((K, rank, sketch), BF16),
        vmem((R, K * rank, rank), BF16),
        vmem((D, C, BL // D, rank), F32),
        vmem((C, D, BL // D, rank), F32),
        vmem((C, BL // D, rank), BF16),
        vmem((C, BL // D, rank), BF16),
        vmem((D, R, BR // D, rank), F32),
        vmem((R, D, BR // D, rank), F32),
        vmem((R, BR // D, rank), BF16),
        vmem((R, BR // D, rank), BF16),
        dma((7,)), dma((6,)),
        dma((C, K)), dma((3, KN - KQ)), dma((2, 4, KM)), dma((2,)), dma((2,)), dma((1,)), dma((1,)), dma((KM,)),
        dma((1,)), dma((C, 2)), dma((3, 2)), dma((C,)), dma((C,)), dma((R,)), dma((R,)),
    ]
    whole = pl.BlockSpec(memory_space=pltpu.VMEM)
    out = jax.ShapeDtypeStruct((BL * C // D, rank), BF16)
    range_rows, corange_rows = pl.pallas_call(
        functools.partial(kernel, (R, C, D, K)),
        out_shape=(out, out),
        in_specs=[pl.BlockSpec(memory_space=pltpu.HBM)] * 7,
        out_specs=(whole, whole),
        scratch_shapes=scratch,
        compiler_params=pltpu.CompilerParams(
            collective_id=0, has_side_effects=True, vmem_limit_bytes=36 * 1024 * 1024
        ),
    )(*[
        pltpu.with_memory_space_constraint(x, pltpu.HBM)
        for x in (left_outer[0], left_inner[0], right_outer[0], right_inner[0],
                  range_test[0], corange_test[0], product_mask)
    ])
    return range_rows[None, None].astype(F32), corange_rows[None, None].astype(F32)


def solution(mesh):
    sizes = tuple(mesh.shape[name] for name in ("row", "col", "depth"))
    return jax.shard_map(
        functools.partial(body, sizes),
        mesh=mesh,
        in_specs=(
            P("row", "depth", "col", None),
            P("row", "depth", "col", None),
            P("col", "depth", "row", None),
            P("col", "depth", "row", None),
            P("col", "row", None),
            P("row", "col", None),
            P("row", "col", "depth"),
        ),
        out_specs=(P("row", "col", "depth", None), P("row", "col", "depth", None)),
        check_vma=False,
    )
```

```python
import functools

import jax
import jax.numpy as jnp
from jax import lax
from jax.experimental import pallas as pl
from jax.experimental.pallas import tpu as pltpu
from jax.sharding import PartitionSpec as P

F32 = jnp.float32
BF16 = jnp.bfloat16
HIGHEST = lax.Precision.HIGHEST
MESH = pl.DeviceIdType.MESH
RULER = 32768


def mm(a, b, contract=(1, 0), precision=None):
    dims = (((contract[0],), (contract[1],)), ((), ()))
    return lax.dot_general(a, b, dims, precision=precision, preferred_element_type=F32)


def mm_split(a, b):
    a_up, b_up = a.astype(BF16), b.astype(BF16)
    a_low, b_low = (a - a_up.astype(F32)).astype(BF16), (b - b_up.astype(F32)).astype(BF16)
    return mm(jnp.concatenate([a_up, a_up, a_low], axis=1), jnp.concatenate([b_up, b_low, b_up], axis=0))


def inverse_schedule(rank):
    low = 1.0 / (rank / 0.05 + 1.0)
    low *= 0.999
    start = 2.0 / (1.0 + low)
    err = 1.0 - low * start
    scales = []
    while err > 1e-3:
        scales.append(2.0 / (2.0 - err * err))
        err = err * err / (2.0 - err * err)
    return start, scales


def kernel(
    sizes,
    lo_h, li_h, ro_h, ri_h, rt_h, ct_h, mask_h,
    out_range, out_corange,
    mask, ruler, lo, ro, ri, rt, ct, lig, rig, rx, qx, ex, tp, tpe, tps, tpo, test, tmid, pps, ppr, probe,
    cx, xs, xr, cps, cpr, crt, clt, zz, rps, rpr, rsend, rout, qps, qpr, qsend, qout,
    load_s, send_s, li_in, ri_in, ext_in, tp_in, te_in, pp_in, pr_in, xr_in, cp_in, cr_in, z_in,
    rp_in, ro_in, qp_in, qo_in,
):
    R, C, D, K = sizes
    KM = K // 2
    KN = K - KM
    KQ = KN // 2
    KR = K // R
    rank = lo_h.shape[2]
    r, c, d = lax.axis_index("row"), lax.axis_index("col"), lax.axis_index("depth")
    is_end = jnp.logical_or(c == 0, c == C - 1)
    is_mid = jnp.logical_not(is_end)
    across = (r + 1 - 2 * lax.rem(r, 2), lax.rem(r + 2, R), R - 1 - r)
    sent = {}

    def send(branch, src, dst, recv, dev, size, sem=0):
        op = pltpu.make_async_remote_copy(
            src_ref=src, dst_ref=dst, send_sem=send_s.at[sem], recv_sem=recv,
            device_id=dev, device_id_type=MESH,
        )
        op.start()
        sent[branch] = sent.get(branch, 0) + size

    def arrive(ref, recv):
        pltpu.make_async_remote_copy(
            src_ref=ref, dst_ref=ref, send_sem=send_s.at[0], recv_sem=recv,
            device_id=(r, c, d), device_id_type=MESH,
        ).wait_recv()

    def drain(sem, ref):
        pltpu.make_async_remote_copy(
            src_ref=ref, dst_ref=ref, send_sem=send_s.at[sem], recv_sem=load_s.at[0],
            device_id=(r, c, d), device_id_type=MESH,
        ).wait_send()

    def bytes_of(size):
        return ruler.at[pl.ds(0, size // (2 * rank))]

    def load(src, dst, index):
        op = pltpu.make_async_copy(src, dst, load_s.at[index])
        op.start()
        return op

    bar = pltpu.get_barrier_semaphore()

    def greet(row, col, depth):
        pl.semaphore_signal(bar, inc=1, device_id=(row, col, depth), device_id_type=MESH)

    def greet_depth(row, col, own):
        if D <= 4:
            for e in range(1 if own else 0, D):
                greet(row, col, lax.rem(d + e, D))
        else:
            @pl.loop(1 if own else 0, D)
            def _(e):
                greet(row, col, lax.rem(d + e, D))

    greet_depth(r, c, True)
    for o in range(1, R):
        greet_depth(lax.rem(r + o, R), c, False)
    for o in range(1, C):
        greet_depth(r, lax.rem(c + o, C), False)
    load_ri = load(ri_h, ri, 0)
    load_ct = load(ct_h, ct, 1)
    for k in range(K):
        load(lo_h.at[k], lo.at[:, pl.ds(k * rank, rank)], 2)
    load_rt = load(rt_h, rt, 3)
    for k in range(K):
        load(ro_h.at[k], ro.at[:, pl.ds(k * rank, rank)], 4)
    load_li = load(li_h, lig.at[c], 5)
    load_mask = load(mask_h, mask, 6)

    pl.semaphore_wait(bar, R * D + C * D - D - 1)

    BLK = lig.shape[2] * rank * 2
    SQ = rank * rank * 2
    sketch = ct_h.shape[1]
    near = 1 + (c // (C - 1)) * (C - 3)
    edge = ((c - 1) // max(C - 3, 1)) * (C - 1)
    other = C - 1 - c
    half = KM * rank

    def send_li(branch, k, owner, dev, src=None):
        send(branch, lig.at[owner, k] if src is None else src, lig.at[owner, k],
             li_in.at[owner, k], dev, BLK)

    def send_ri(branch, k, owner, to, slot):
        send(branch, rig.at[owner, k - KQ], rig.at[owner, k - KQ], ri_in.at[slot, k - KQ], (to, c, d), BLK)

    def relay_ri(branch, k):
        via, to = (0, 1) if k % 2 == 0 else (1, 0)
        arrive(rig.at[across[via], k - KQ], ri_in.at[via, k - KQ])
        send_ri(branch, k, across[via], across[to], 2)

    def wait_ri(k, skip):
        for slot in range(3):
            if slot != skip:
                arrive(rig.at[across[slot], k - KQ], ri_in.at[slot, k - KQ])

    def via_of(k):
        return 0 if k % 2 == 0 else 1

    def tall(ref_row, kk, part):
        return rx.at[ref_row, kk, pl.ds(part * rank, rank)]

    def send_x(branch, kk, part, owner, to, slot):
        send(branch, tall(owner, kk, part), tall(owner, kk, part), ext_in.at[part, slot, kk],
             (to, c, d), BLK)

    def relay_x(branch, kk, part):
        via, to = (0, 1) if (kk + part) % 2 == 0 else (1, 0)
        arrive(tall(across[via], kk, part), ext_in.at[part, via, kk])
        send_x(branch, kk, part, across[via], across[to], 2)

    def wait_x(kk, part):
        for slot in range(3):
            if slot != (kk + part) % 2:
                arrive(tall(across[slot], kk, part), ext_in.at[part, slot, kk])

    def cross_tall(kk, k, to):
        total = None
        for b in range(C):
            term = mm(rx[b, kk], lig[b, k])
            total = term if total is None else total + term
        xs[kk] = total[rank:].astype(BF16)
        send("mid" if k >= KN else "end", xs.at[kk], xr.at[kk], xr_in.at[kk], (r, to, d), SQ)
        cx[k] = total[:rank].astype(BF16)

    def tests():
        load_ct.wait()
        pltpu.make_async_copy(lo, lo, load_s.at[2]).wait()
        tp[...] = mm(ct[...].T, lo[...]).astype(BF16)

    def probes(branch):
        load_rt.wait()
        pltpu.make_async_copy(ro, ro, load_s.at[4]).wait()
        part = mm(rt[...].T, ro[...])
        for n in range(R):
            pps[n] = part[:, n * KR * rank:(n + 1) * KR * rank]
        for slot in range(3):
            send(branch, pps.at[across[slot]], ppr.at[slot], pp_in.at[0],
                 (across[slot], c, d), KR * SQ * 2)

    def probe_sum(branch):
        arrive(ppr, pp_in.at[0])
        total = pps[r]
        for slot in range(3):
            total = total + ppr[slot]
        probe[r] = total.astype(BF16)
        for slot in range(3):
            send(branch, probe.at[r], probe.at[r], pr_in.at[0], (across[slot], c, d), KR * SQ)

    def probe_wait():
        arrive(probe.at[pl.ds(0, 3)], pr_in.at[0])

    scale = (K * D) ** -0.5

    def cross_plain(k):
        total = None
        for b in range(C):
            term = mm(rig[b, k - KQ], lig[b, k])
            total = term if total is None else total + term
        return total.astype(BF16)

    def right_of(k, cross):
        weight = mask[0, 0, k].astype(F32) * scale
        lanes = pl.ds(k % KR * rank, rank)
        right = (mm(probe[k // KR, :, lanes], cross) * weight).astype(BF16)
        crt[c, :, pl.ds(k * rank, rank)] = right

    def part_of(n, part):
        return crt.at[n, :, pl.ds(0, KN * rank) if part == 0 else pl.ds(KN * rank, half)]

    def send_crt(branch, owner, part, to):
        send(branch, part_of(owner, part), part_of(owner, part), cr_in.at[owner, part],
             (r, to, d), (KN if part == 0 else KM) * SQ)

    @pl.when(is_mid)
    def _():
        B = "mid"
        for k in range(K):
            send_li(B, k, c, (r, other, d), li_h.at[k])
            if k < KN:
                send_li(B, k, c, (r, edge, d), li_h.at[k])
        load_ri.wait()
        for k in range(KQ):
            qx[k] = ri[k].T
            send(B, qx.at[k], tall(r, k, 1), ext_in.at[1, 3, k], (r, edge, d), BLK)
        for k in range(KQ, KN):
            rig[r, k - KQ] = ri[k].T
            for slot in range(2):
                send_ri(B, k, r, across[slot], slot)
        for kk in range(KM):
            rx[r, kk, 0:rank] = ri[KN + kk].T
            for slot in range(2):
                send_x(B, kk, 0, r, across[slot], slot)
        tests()
        probes(B)
        far = C - 1 - edge
        lower = c == 1
        h = jnp.where(lower, 0, 1)
        arrive(lig.at[edge, 0], li_in.at[edge, 0])
        send_li(B, 0, edge, (r, other, d))
        for k in range(KN):
            arrive(lig.at[other, k], li_in.at[other, k])
            send_li(B, k, other, (r, edge, d))
            if k >= KQ:
                relay_ri(B, k)
        relay_x(B, 0, 0)
        arrive(tpe, tp_in.at[0])
        both = tpe[...].astype(F32) + tp[...].astype(F32)
        tmid[...] = jnp.where(lower, both[:, 0:half], both[:, half:2 * half])
        tps[...] = jnp.where(lower, both[:, half:2 * half], both[:, 0:half]).astype(BF16)
        send(B, tps, tpo, tp_in.at[1], (r, other, d), sketch * half * 2)
        relay_x(B, 1, 0)
        for k in range(1, KN):
            arrive(lig.at[edge, k], li_in.at[edge, k])
            send_li(B, k, edge, (r, other, d))
        probe_sum(B)
        arrive(tall(r, 0, 1), ext_in.at[1, 3, 0])
        for slot in range(2):
            send_x(B, 0, 1, r, across[slot], slot)
        arrive(lig.at[far, 0], li_in.at[far, 0])
        send_li(B, 0, far, (r, edge, d))
        arrive(tpo, tp_in.at[1])
        test[h] = (tmid[...] + tpo[...].astype(F32)).astype(BF16)
        for to in (edge, other):
            send(B, test.at[h], test.at[h], te_in.at[h], (r, to, d), sketch * half * 2)
        arrive(tall(r, 1, 1), ext_in.at[1, 3, 1])
        for slot in range(2):
            send_x(B, 1, 1, r, across[slot], slot)
        arrive(lig.at[edge, KN], li_in.at[edge, KN])
        send_li(B, KN, edge, (r, other, d))
        for k in range(1, KN):
            arrive(lig.at[far, k], li_in.at[far, k])
            send_li(B, k, far, (r, edge, d))
        relay_x(B, 0, 1)
        for k in range(KN + 1, K):
            arrive(lig.at[edge, k], li_in.at[edge, k])
            send_li(B, k, edge, (r, other, d))
        arrive(test.at[1 - h], te_in.at[1 - h])
        send(B, test.at[1 - h], test.at[1 - h], te_in.at[1 - h], (r, edge, d), sketch * half * 2)
        for kk in range(1, KM):
            relay_x(B, kk, 1)
        for k in range(KQ, KN):
            wait_ri(k, via_of(k))
        load_li.wait()
        load_mask.wait()
        for k in range(KQ, KN):
            cx[k] = cross_plain(k)
        probe_wait()
        for k in range(KQ, KN):
            right_of(k, cx[k])
        for k in range(KQ):
            arrive(xr.at[k], xr_in.at[k])
            cx[k] = xr[k]
            right_of(k, cx[k])
        send_crt(B, c, 0, other)
        send_crt(B, c, 0, edge)
        for kk in range(KM):
            for part in range(2):
                wait_x(kk, part)
            for b in (other, far):
                arrive(lig.at[b, KN + kk], li_in.at[b, KN + kk])
            cross_tall(kk, KN + kk, edge)
        for k in range(KN, K):
            right_of(k, cx[k])
        send_crt(B, c, 1, other)

    @pl.when(is_end)
    def _():
        B = "end"
        send_li(B, 0, c, (r, near, d), li_h.at[0])
        load_ri.wait()
        for k in range(KQ):
            rx[r, k, 0:rank] = ri[k].T
            for slot in range(2):
                send_x(B, k, 0, r, across[slot], slot)
        for k in range(KQ, KN):
            rig[r, k - KQ] = ri[k].T
            for slot in range(2):
                send_ri(B, k, r, across[slot], slot)
        tests()
        send(B, tp, tpe, tp_in.at[0], (r, near, d), sketch * K * rank * 2)
        for k in range(1, KN):
            send_li(B, k, c, (r, near, d), li_h.at[k])
        for kk in range(KM):
            ex[kk] = ri[KN + kk].T
            send(B, ex.at[kk], tall(r, kk, 1), ext_in.at[1, 3, kk], (r, near, d), BLK)
        for k in range(KN, K):
            send_li(B, k, c, (r, near, d), li_h.at[k])
        probes(B)
        for k in range(KQ):
            relay_x(B, k, 0)
        for k in range(KQ, KN):
            relay_ri(B, k)
        for k in range(KQ):
            arrive(tall(r, k, 1), ext_in.at[1, 3, k])
            for slot in range(2):
                send_x(B, k, 1, r, across[slot], slot)
        probe_sum(B)
        for k in range(KQ):
            relay_x(B, k, 1)
        load_li.wait()
        load_mask.wait()
        probe_wait()
        for k in range(KQ):
            for part in range(2):
                wait_x(k, part)
            for n in (near, C - 1 - near, other):
                arrive(lig.at[n, k], li_in.at[n, k])
            cross_tall(k, k, near)
            right_of(k, cx[k])
        for k in range(KQ, KN):
            wait_ri(k, via_of(k))
            for n in (near, C - 1 - near, other):
                arrive(lig.at[n, k], li_in.at[n, k])
            cx[k] = cross_plain(k)
            right_of(k, cx[k])
        send_crt(B, c, 0, near)
        for h in range(2):
            arrive(test.at[h], te_in.at[h])
        for kk in range(KM):
            arrive(xr.at[kk], xr_in.at[kk])
            cx[KN + kk] = xr[kk]
            right_of(KN + kk, xr[kk])
        for to in (other, C - 1 - near, near):
            send_crt(B, c, 1, to)

    core_part = None
    for k in range(K):
        weight = mask[0, 0, k].astype(F32) * scale
        hk, kk = (0, k) if k < KN else (1, k - KN)
        test_k = test[hk, :, kk * rank:(kk + 1) * rank]
        clt[k] = (mm(cx[k], test_k, (1, 1)) * weight).astype(BF16)
        term = mm(crt[c, :, k * rank:(k + 1) * rank], test_k, (1, 1))
        core_part = term if core_part is None else core_part + term
    cps[...] = core_part
    for o in range(1, D):
        send("cp", cps, cpr.at[d], cp_in.at[0], (r, c, lax.rem(d + o, D)), 0, 3)
    cpr[d] = core_part

    @pl.when(is_mid)
    def _():
        B = "mid"
        arrive(part_of(edge, 0), cr_in.at[edge, 0])
        send_crt(B, edge, 0, other)

    arrive(cpr.at[pl.ds(0, D - 1)], cp_in.at[0])
    core = cpr[0]
    for n in range(1, D):
        core = core + cpr[n]

    def relay_other(part):
        arrive(part_of(other, part), cr_in.at[other, part])
        send_crt("mid", other, part, edge)


    @pl.when(is_mid)
    def _():
        relay_other(0)

    gram = mm(core, core, (1, 1), HIGHEST)
    eye = (
        lax.broadcasted_iota(jnp.int32, (rank, rank), 0)
        == lax.broadcasted_iota(jnp.int32, (rank, rank), 1)
    ).astype(F32)
    trace = jnp.sum(core * core)
    ridge = 0.05 * trace / rank + 1e-05
    norm = 1.0 / jnp.broadcast_to(trace + ridge, (rank, rank))
    gram = (gram + ridge * eye) * norm
    start, scales = inverse_schedule(rank)
    rest = eye - start * gram
    inv = (scales[0] * start) * (eye + rest)
    rest = (1.0 - scales[0]) * eye + scales[0] * mm_split(rest, rest)
    for step, factor in enumerate(scales[1:]):
        if step == 5:

            @pl.when(is_mid)
            def _():
                send_crt("mid", c, 1, edge)

        both = mm_split(jnp.concatenate([inv, rest], axis=0), rest)
        inv = factor * (inv + both[:rank])
        rest = (1.0 - factor) * eye + factor * both[rank:]
    solved = mm_split(inv, core)
    solved = solved + mm_split(inv, core - mm(gram, solved, precision=HIGHEST))
    weights = (solved * (norm[:, 0:1] * rank**0.5)).astype(BF16)

    rows = KN * rank

    def zpart(n, part):
        return zz.at[n, pl.ds(0, rows) if part == 0 else pl.ds(rows, half)]

    def send_z(slot, part):
        send("all", zpart(r, part), zpart(r, part), z_in.at[slot, part], (across[slot], c, d),
             (KN if part == 0 else KM) * SQ)

    for part in range(2):
        for k in range(KN) if part == 0 else range(KN, K):
            zz[r, pl.ds(k * rank, rank)] = mm(clt[k], weights, (1, 1)).astype(BF16)
        send_z(part, part)
    for part in range(2):
        send_z(1 - part, part)

    @pl.when(is_mid)
    def _():
        B = "mid"
        far = C - 1 - edge
        relay_other(1)
        arrive(part_of(far, 0), cr_in.at[far, 0])
        send_crt(B, far, 0, edge)

    def relay_z(part, branch):
        via, to = (0, 1) if part == 0 else (1, 0)
        arrive(zpart(across[via], part), z_in.at[via, part])
        send(branch, zpart(across[via], part), zpart(across[via], part), z_in.at[2, part],
             (across[to], c, d), (KN if part == 0 else KM) * SQ)

    part_l = lo_h.shape[1] // D
    place = c * D + d
    owner, slot_l = place // C, lax.rem(place, C)

    def halves(left, right, contract, parts, got, sem, in_s, index):
        size = left.shape[0] // D
        if D == 2:
            for n in (1 - d, d):
                rows = left[pl.ds(pl.multiple_of(n * size, size), size), :]
                parts[n, index] = mm(rows, right, contract)
                if n is not d:
                    send(sem[0], parts.at[n, index], got.at[index, d], in_s.at[index], (r, c, n), 0, sem[1])
        else:
            total = mm(left[...], right, contract)
            for n in range(D):
                parts[n, index] = total[n * size:(n + 1) * size]
            for e in range(1, D):
                n = lax.rem(d + e, D)
                send(sem[0], parts.at[n, index], got.at[index, d], in_s.at[index], (r, c, n), 0, sem[1])

    def range_mm(j, index):
        halves(lo, crt[j], (1, 1), rps, rpr, ("rp", 4), rp_in, index)

    def range_out(j, index, first, branch="all"):
        total = rps[d, index]
        arrive(rpr.at[index, pl.ds(0, D - 1)], rp_in.at[index])
        for e in range(1, D):
            total = total + rpr[index, lax.rem(d + e, D)]
        rsend[index] = total.astype(BF16)
        if first:
            @pl.when(owner != d)
            def _():
                send("ro", rsend.at[index], rout.at[slot_l], ro_in.at[slot_l], (r, j, owner), part_l * rank * 2, 1)
        else:
            send(branch, rsend.at[index], rout.at[slot_l], ro_in.at[slot_l], (r, j, owner), part_l * rank * 2)

    part_r = ro_h.shape[1] // D
    place_q = r * D + d
    owner_q, slot_q = place_q // R, lax.rem(place_q, R)

    def corange_mm(i, index):
        halves(ro, zz[i], (1, 0), qps, qpr, ("qp", 5), qp_in, index)

    def corange_out(i, index, first):
        total = qps[d, index]
        arrive(qpr.at[index, pl.ds(0, D - 1)], qp_in.at[index])
        for e in range(1, D):
            total = total + qpr[index, lax.rem(d + e, D)]
        qsend[index] = total.astype(BF16)
        if first:
            @pl.when(owner_q != d)
            def _():
                send("qo", qsend.at[index], qout.at[slot_q], qo_in.at[slot_q], (i, c, owner_q), part_r * rank * 2, 2)
        else:
            send("all", qsend.at[index], qout.at[slot_q], qo_in.at[slot_q], (i, c, owner_q), part_r * rank * 2)

    order = (c, jnp.where(is_end, near, other), jnp.where(is_end, C - 1 - near, C - 1 - edge),
             jnp.where(is_end, other, edge))

    range_mm(c, 0)

    @pl.when(is_end)
    def _():
        for part in range(2):
            arrive(part_of(near, part), cr_in.at[near, part])

    range_mm(order[1], 1)

    @pl.when(is_end)
    def _():
        for part in range(2):
            arrive(part_of(C - 1 - near, part), cr_in.at[C - 1 - near, part])
        range_mm(order[2], 2)
        relay_z(0, "end")
        relay_z(1, "end")

    @pl.when(is_mid)
    def _():
        relay_z(0, "mid")
        relay_z(1, "mid")

    for index in range(2):
        range_out(order[index], index, index == 0)
    corange_mm(r, 0)

    @pl.when(is_end)
    def _():
        range_out(order[2], 2, False, "end")
        for part in range(2):
            arrive(part_of(other, part), cr_in.at[other, part])

    @pl.when(is_mid)
    def _():
        for n in (C - 1 - edge, edge):
            arrive(part_of(n, 1), cr_in.at[n, 1])
        range_mm(order[2], 2)

    range_mm(order[3], 3)
    arrive(zpart(across[0], 1), z_in.at[0, 1])
    corange_mm(across[0], 1)
    arrive(zpart(across[1], 0), z_in.at[1, 0])
    corange_mm(across[1], 2)

    @pl.when(is_mid)
    def _():
        range_out(order[2], 2, False, "mid")

    range_out(order[3], 3, False)
    corange_out(r, 0, True)
    for slot in range(2):
        corange_out(across[slot], slot + 1, False)
    for part in range(2):
        arrive(zpart(across[2], part), z_in.at[2, part])
    corange_mm(across[2], 3)
    corange_out(across[2], 3, False)

    @pl.when(owner == d)
    def _():
        rout[slot_l] = rsend[0]

    @pl.when(owner_q == d)
    def _():
        qout[slot_q] = qsend[0]

    for q in range(C):
        src = d * C + q
        mine = jnp.logical_and(src // D == c, lax.rem(src, D) == d)

        @pl.when(jnp.logical_not(mine))
        def _(q=q):
            arrive(rout.at[q], ro_in.at[q])

        out_range[q * part_l:(q + 1) * part_l, :] = rout[q]
    for q in range(R):
        src = d * R + q
        mine = jnp.logical_and(src // D == r, lax.rem(src, D) == d)

        @pl.when(jnp.logical_not(mine))
        def _(q=q):
            arrive(qout.at[q], qo_in.at[q])

        out_corange[q * part_r:(q + 1) * part_r, :] = qout[q]

    drain(3, cpr.at[pl.ds(0, D - 1)])
    drain(4, rpr.at[:, pl.ds(0, D - 1)])
    drain(5, qpr.at[:, pl.ds(0, D - 1)])
    for branch, cond in (("mid", is_mid), ("end", is_end)):
        @pl.when(cond)
        def _(branch=branch):
            drain(0, bytes_of(sent["all"] + sent[branch]))
    for branch, cond, sem in (("ro", owner != d, 1), ("qo", owner_q != d, 2)):
        @pl.when(cond)
        def _(branch=branch, sem=sem):
            drain(sem, bytes_of(sent[branch]))


def body(sizes, left_outer, left_inner, right_outer, right_inner, range_test, corange_test, product_mask):
    R, C, D = sizes
    K, BL, rank = left_outer.shape[1:]
    BR = right_outer.shape[2]
    sketch = corange_test.shape[2]
    assert R == 4 and C == 4 and K % R == 0 and BL == BR and BL % D == 0 and D > 1
    KM = K // 2
    KN = K - KM
    KQ = KN // 2
    KR = K // R
    dma = pltpu.SemaphoreType.DMA
    vmem = pltpu.VMEM
    scratch = [
        pltpu.SMEM((1, 1, K), jnp.int32),
        vmem((RULER, rank), BF16),
        vmem((BL, K * rank), BF16),
        vmem((BR, K * rank), BF16),
        vmem((K, BR, rank), BF16),
        vmem((BR, rank), BF16),
        vmem((BL, sketch), BF16),
        vmem((C, K, BL, rank), BF16),
        vmem((R, KN - KQ, rank, BR), BF16),
        vmem((R, KM, 2 * rank, BR), BF16),
        vmem((KQ, rank, BR), BF16),
        vmem((KM, rank, BR), BF16),
        vmem((sketch, K * rank), BF16),
        vmem((sketch, K * rank), BF16),
        vmem((sketch, KM * rank), BF16),
        vmem((sketch, KM * rank), BF16),
        vmem((2, sketch, KM * rank), BF16),
        vmem((sketch, KM * rank), F32),
        vmem((R, rank, KR * rank), F32),
        vmem((R - 1, rank, KR * rank), F32),
        vmem((R, rank, KR * rank), BF16),
        vmem((K, rank, rank), BF16),
        vmem((KM, rank, rank), BF16),
        vmem((KM, rank, rank), BF16),
        vmem((rank, sketch), F32),
        vmem((D, rank, sketch), F32),
        vmem((C, rank, K * rank), BF16),
        vmem((K, rank, sketch), BF16),
        vmem((R, K * rank, rank), BF16),
        vmem((D, C, BL // D, rank), F32),
        vmem((C, D, BL // D, rank), F32),
        vmem((C, BL // D, rank), BF16),
        vmem((C, BL // D, rank), BF16),
        vmem((D, R, BR // D, rank), F32),
        vmem((R, D, BR // D, rank), F32),
        vmem((R, BR // D, rank), BF16),
        vmem((R, BR // D, rank), BF16),
        dma((7,)), dma((6,)),
        dma((C, K)), dma((3, KN - KQ)), dma((2, 4, KM)), dma((2,)), dma((2,)), dma((1,)), dma((1,)), dma((KM,)),
        dma((1,)), dma((C, 2)), dma((3, 2)), dma((C,)), dma((C,)), dma((R,)), dma((R,)),
    ]
    whole = pl.BlockSpec(memory_space=pltpu.VMEM)
    out = jax.ShapeDtypeStruct((BL * C // D, rank), BF16)
    range_rows, corange_rows = pl.pallas_call(
        functools.partial(kernel, (R, C, D, K)),
        out_shape=(out, out),
        in_specs=[pl.BlockSpec(memory_space=pltpu.HBM)] * 7,
        out_specs=(whole, whole),
        scratch_shapes=scratch,
        compiler_params=pltpu.CompilerParams(
            collective_id=0, has_side_effects=True, vmem_limit_bytes=36 * 1024 * 1024
        ),
    )(*[
        pltpu.with_memory_space_constraint(x, pltpu.HBM)
        for x in (left_outer[0], left_inner[0], right_outer[0], right_inner[0],
                  range_test[0], corange_test[0], product_mask)
    ])
    return range_rows[None, None].astype(F32), corange_rows[None, None].astype(F32)


def solution(mesh):
    sizes = tuple(mesh.shape[name] for name in ("row", "col", "depth"))
    return jax.shard_map(
        functools.partial(body, sizes),
        mesh=mesh,
        in_specs=(
            P("row", "depth", "col", None),
            P("row", "depth", "col", None),
            P("col", "depth", "row", None),
            P("col", "depth", "row", None),
            P("col", "row", None),
            P("row", "col", None),
            P("row", "col", "depth"),
        ),
        out_specs=(P("row", "col", "depth", None), P("row", "col", "depth", None)),
        check_vma=False,
    )
```

```python
import functools

import jax
import jax.numpy as jnp
from jax import lax
from jax.experimental import pallas as pl
from jax.experimental.pallas import tpu as pltpu
from jax.sharding import PartitionSpec as P

F32 = jnp.float32
BF16 = jnp.bfloat16
HIGHEST = lax.Precision.HIGHEST
MESH = pl.DeviceIdType.MESH
RULER = 32768


def mm(a, b, contract=(1, 0), precision=None):
    dims = (((contract[0],), (contract[1],)), ((), ()))
    return lax.dot_general(a, b, dims, precision=precision, preferred_element_type=F32)


def mm_split(a, b):
    a_up, b_up = a.astype(BF16), b.astype(BF16)
    a_low, b_low = (a - a_up.astype(F32)).astype(BF16), (b - b_up.astype(F32)).astype(BF16)
    return mm(jnp.concatenate([a_up, a_up, a_low], axis=1), jnp.concatenate([b_up, b_low, b_up], axis=0))


def inverse_schedule(rank):
    low = 1.0 / (rank / 0.05 + 1.0)
    low *= 0.999
    start = 2.0 / (1.0 + low)
    err = 1.0 - low * start
    scales = []
    while err > 1e-3:
        scales.append(2.0 / (2.0 - err * err))
        err = err * err / (2.0 - err * err)
    return start, scales


def kernel(
    sizes,
    lo_h, li_h, ro_h, ri_h, rt_h, ct_h, mask_h,
    out_range, out_corange,
    mask, ruler, lo, ro, ri, rt, ct, lig, rig, rx, qx, ex, tp, tpe, tps, tpo, test, tmid, pps, ppr, probe,
    cx, xs, xr, cps, cpr, crt, clt, zz, rps, rpr, rsend, rout, qps, qpr, qsend, qout,
    load_s, send_s, li_in, ri_in, ext_in, cp_in, cr_in, z_in,
    rp_in, ro_in, qp_in, qo_in,
):
    R, C, D, K = sizes
    KM = K // 2
    KN = K - KM
    KQ = KN // 2
    KR = K // R
    rank = lo_h.shape[2]
    r, c, d = lax.axis_index("row"), lax.axis_index("col"), lax.axis_index("depth")
    is_end = jnp.logical_or(c == 0, c == C - 1)
    is_mid = jnp.logical_not(is_end)
    across = (r + 1 - 2 * lax.rem(r, 2), lax.rem(r + 2, R), R - 1 - r)
    sent = {}

    def send(branch, src, dst, recv, dev, size, sem=0):
        op = pltpu.make_async_remote_copy(
            src_ref=src, dst_ref=dst, send_sem=send_s.at[sem], recv_sem=recv,
            device_id=dev, device_id_type=MESH,
        )
        op.start()
        sent[branch] = sent.get(branch, 0) + size

    def arrive(ref, recv):
        pltpu.make_async_remote_copy(
            src_ref=ref, dst_ref=ref, send_sem=send_s.at[0], recv_sem=recv,
            device_id=(r, c, d), device_id_type=MESH,
        ).wait_recv()

    def drain(sem, ref):
        pltpu.make_async_remote_copy(
            src_ref=ref, dst_ref=ref, send_sem=send_s.at[sem], recv_sem=load_s.at[0],
            device_id=(r, c, d), device_id_type=MESH,
        ).wait_send()

    def bytes_of(size):
        return ruler.at[pl.ds(0, size // (2 * rank))]

    def load(src, dst, index):
        op = pltpu.make_async_copy(src, dst, load_s.at[index])
        op.start()
        return op

    bar = pltpu.get_barrier_semaphore()

    def greet(row, col, depth):
        pl.semaphore_signal(bar, inc=1, device_id=(row, col, depth), device_id_type=MESH)

    def greet_depth(row, col, own):
        if D <= 4:
            for e in range(1 if own else 0, D):
                greet(row, col, lax.rem(d + e, D))
        else:
            @pl.loop(1 if own else 0, D)
            def _(e):
                greet(row, col, lax.rem(d + e, D))

    greet_depth(r, c, True)
    for o in range(1, R):
        greet_depth(lax.rem(r + o, R), c, False)
    for o in range(1, C):
        greet_depth(r, lax.rem(c + o, C), False)
    load_ri = load(ri_h, ri, 0)
    load_ct = load(ct_h, ct, 1)
    for k in range(K):
        load(lo_h.at[k], lo.at[:, pl.ds(k * rank, rank)], 2)
    load_rt = load(rt_h, rt, 3)
    for k in range(K):
        load(ro_h.at[k], ro.at[:, pl.ds(k * rank, rank)], 4)
    load_li = load(li_h, lig.at[c], 5)
    load_mask = load(mask_h, mask, 6)

    pl.semaphore_wait(bar, R * D + C * D - D - 1)

    BLK = lig.shape[2] * rank * 2
    SQ = rank * rank * 2
    sketch = ct_h.shape[1]
    near = 1 + (c // (C - 1)) * (C - 3)
    edge = ((c - 1) // max(C - 3, 1)) * (C - 1)
    other = C - 1 - c
    half = KM * rank

    def send_li(branch, k, owner, dev, src=None):
        send(branch, lig.at[owner, k] if src is None else src, lig.at[owner, k],
             li_in.at[owner, k], dev, BLK)

    def send_ri(branch, k, owner, to, slot):
        send(branch, rig.at[owner, k - KQ], rig.at[owner, k - KQ], ri_in.at[slot, k - KQ], (to, c, d), BLK)

    def relay_ri(branch, k):
        via, to = (0, 1) if k % 2 == 0 else (1, 0)
        arrive(rig.at[across[via], k - KQ], ri_in.at[via, k - KQ])
        send_ri(branch, k, across[via], across[to], 2)

    def wait_ri(k, skip):
        for slot in range(3):
            if slot != skip:
                arrive(rig.at[across[slot], k - KQ], ri_in.at[slot, k - KQ])

    def via_of(k):
        return 0 if k % 2 == 0 else 1

    def tall(ref_row, kk, part):
        return rx.at[ref_row, kk, pl.ds(part * rank, rank)]

    def send_x(branch, kk, part, owner, to, slot):
        send(branch, tall(owner, kk, part), tall(owner, kk, part), ext_in.at[part, slot, kk],
             (to, c, d), BLK)

    def relay_x(branch, kk, part):
        via, to = (0, 1) if (kk + part) % 2 == 0 else (1, 0)
        arrive(tall(across[via], kk, part), ext_in.at[part, via, kk])
        send_x(branch, kk, part, across[via], across[to], 2)

    def wait_x(kk, part):
        for slot in range(3):
            if slot != (kk + part) % 2:
                arrive(tall(across[slot], kk, part), ext_in.at[part, slot, kk])

    def cross_tall(kk, k, to):
        total = None
        for b in range(C):
            term = mm(rx[b, kk], lig[b, k])
            total = term if total is None else total + term
        xs[kk] = total[rank:].astype(BF16)
        send("mid" if k >= KN else "end", xs.at[kk], xr.at[kk], li_in.at[to, kk], (r, to, d), SQ)
        cx[k] = total[:rank].astype(BF16)

    def tests():
        load_ct.wait()
        pltpu.make_async_copy(lo, lo, load_s.at[2]).wait()
        tp[...] = mm(ct[...].T, lo[...]).astype(BF16)

    def probes(branch):
        load_rt.wait()
        pltpu.make_async_copy(ro, ro, load_s.at[4]).wait()
        part = mm(rt[...].T, ro[...])
        for n in range(R):
            pps[n] = part[:, n * KR * rank:(n + 1) * KR * rank]
        for slot in range(3):
            send(branch, pps.at[across[slot]], ppr.at[slot], cr_in.at[c, 0],
                 (across[slot], c, d), KR * SQ * 2)

    def probe_sum(branch):
        arrive(ppr, cr_in.at[c, 0])
        total = pps[r]
        for slot in range(3):
            total = total + ppr[slot]
        probe[r] = total.astype(BF16)
        for slot in range(3):
            send(branch, probe.at[r], probe.at[r], cr_in.at[c, 1], (across[slot], c, d), KR * SQ)

    def probe_wait():
        arrive(probe.at[pl.ds(0, 3)], cr_in.at[c, 1])

    scale = (K * D) ** -0.5

    def cross_plain(k):
        total = None
        for b in range(C):
            term = mm(rig[b, k - KQ], lig[b, k])
            total = term if total is None else total + term
        return total.astype(BF16)

    def right_of(k, cross):
        weight = mask[0, 0, k].astype(F32) * scale
        lanes = pl.ds(k % KR * rank, rank)
        right = (mm(probe[k // KR, :, lanes], cross) * weight).astype(BF16)
        crt[c, :, pl.ds(k * rank, rank)] = right

    def part_of(n, part):
        return crt.at[n, :, pl.ds(0, KN * rank) if part == 0 else pl.ds(KN * rank, half)]

    def send_crt(branch, owner, part, to):
        send(branch, part_of(owner, part), part_of(owner, part), cr_in.at[owner, part],
             (r, to, d), (KN if part == 0 else KM) * SQ)

    @pl.when(is_mid)
    def _():
        B = "mid"
        for k in range(K):
            send_li(B, k, c, (r, other, d), li_h.at[k])
            if k < KN:
                send_li(B, k, c, (r, edge, d), li_h.at[k])
        load_ri.wait()
        for k in range(KQ):
            qx[k] = ri[k].T
            send(B, qx.at[k], tall(r, k, 1), ext_in.at[1, 3, k], (r, edge, d), BLK)
        for k in range(KQ, KN):
            rig[r, k - KQ] = ri[k].T
            for slot in range(2):
                send_ri(B, k, r, across[slot], slot)
        for kk in range(KM):
            rx[r, kk, 0:rank] = ri[KN + kk].T
            for slot in range(2):
                send_x(B, kk, 0, r, across[slot], slot)
        tests()
        probes(B)
        far = C - 1 - edge
        lower = c == 1
        h = jnp.where(lower, 0, 1)
        arrive(lig.at[edge, 0], li_in.at[edge, 0])
        send_li(B, 0, edge, (r, other, d))
        for k in range(KN):
            arrive(lig.at[other, k], li_in.at[other, k])
            send_li(B, k, other, (r, edge, d))
            if k >= KQ:
                relay_ri(B, k)
        relay_x(B, 0, 0)
        arrive(tpe, li_in.at[c, K - 2])
        both = tpe[...].astype(F32) + tp[...].astype(F32)
        tmid[...] = jnp.where(lower, both[:, 0:half], both[:, half:2 * half])
        tps[...] = jnp.where(lower, both[:, half:2 * half], both[:, 0:half]).astype(BF16)
        send(B, tps, tpo, li_in.at[other, K - 1], (r, other, d), sketch * half * 2)
        relay_x(B, 1, 0)
        for k in range(1, KN):
            arrive(lig.at[edge, k], li_in.at[edge, k])
            send_li(B, k, edge, (r, other, d))
        probe_sum(B)
        arrive(tall(r, 0, 1), ext_in.at[1, 3, 0])
        for slot in range(2):
            send_x(B, 0, 1, r, across[slot], slot)
        arrive(lig.at[far, 0], li_in.at[far, 0])
        send_li(B, 0, far, (r, edge, d))
        arrive(tpo, li_in.at[c, K - 1])
        test[h] = (tmid[...] + tpo[...].astype(F32)).astype(BF16)
        for to in (edge, other):
            send(B, test.at[h], test.at[h], ext_in.at[0, 3, h], (r, to, d), sketch * half * 2)
        arrive(tall(r, 1, 1), ext_in.at[1, 3, 1])
        for slot in range(2):
            send_x(B, 1, 1, r, across[slot], slot)
        arrive(lig.at[edge, KN], li_in.at[edge, KN])
        send_li(B, KN, edge, (r, other, d))
        for k in range(1, KN):
            arrive(lig.at[far, k], li_in.at[far, k])
            send_li(B, k, far, (r, edge, d))
        relay_x(B, 0, 1)
        for k in range(KN + 1, K):
            arrive(lig.at[edge, k], li_in.at[edge, k])
            send_li(B, k, edge, (r, other, d))
        arrive(test.at[1 - h], ext_in.at[0, 3, 1 - h])
        send(B, test.at[1 - h], test.at[1 - h], ext_in.at[0, 3, 1 - h], (r, edge, d), sketch * half * 2)
        for kk in range(1, KM):
            relay_x(B, kk, 1)
        for k in range(KQ, KN):
            wait_ri(k, via_of(k))
        load_li.wait()
        load_mask.wait()
        for k in range(KQ, KN):
            cx[k] = cross_plain(k)
        probe_wait()
        for k in range(KQ, KN):
            right_of(k, cx[k])
        for k in range(KQ):
            arrive(xr.at[k], li_in.at[c, k])
            cx[k] = xr[k]
            right_of(k, cx[k])
        send_crt(B, c, 0, other)
        send_crt(B, c, 0, edge)
        for kk in range(KM):
            for part in range(2):
                wait_x(kk, part)
            for b in (other, far):
                arrive(lig.at[b, KN + kk], li_in.at[b, KN + kk])
            cross_tall(kk, KN + kk, edge)
        for k in range(KN, K):
            right_of(k, cx[k])
        send_crt(B, c, 1, other)

    @pl.when(is_end)
    def _():
        B = "end"
        send_li(B, 0, c, (r, near, d), li_h.at[0])
        load_ri.wait()
        for k in range(KQ):
            rx[r, k, 0:rank] = ri[k].T
            for slot in range(2):
                send_x(B, k, 0, r, across[slot], slot)
        for k in range(KQ, KN):
            rig[r, k - KQ] = ri[k].T
            for slot in range(2):
                send_ri(B, k, r, across[slot], slot)
        tests()
        send(B, tp, tpe, li_in.at[near, K - 2], (r, near, d), sketch * K * rank * 2)
        for k in range(1, KN):
            send_li(B, k, c, (r, near, d), li_h.at[k])
        for kk in range(KM):
            ex[kk] = ri[KN + kk].T
            send(B, ex.at[kk], tall(r, kk, 1), ext_in.at[1, 3, kk], (r, near, d), BLK)
        for k in range(KN, K):
            send_li(B, k, c, (r, near, d), li_h.at[k])
        probes(B)
        for k in range(KQ):
            relay_x(B, k, 0)
        for k in range(KQ, KN):
            relay_ri(B, k)
        for k in range(KQ):
            arrive(tall(r, k, 1), ext_in.at[1, 3, k])
            for slot in range(2):
                send_x(B, k, 1, r, across[slot], slot)
        probe_sum(B)
        for k in range(KQ):
            relay_x(B, k, 1)
        load_li.wait()
        load_mask.wait()
        probe_wait()
        for k in range(KQ):
            for part in range(2):
                wait_x(k, part)
            for n in (near, C - 1 - near, other):
                arrive(lig.at[n, k], li_in.at[n, k])
            cross_tall(k, k, near)
            right_of(k, cx[k])
        for k in range(KQ, KN):
            wait_ri(k, via_of(k))
            for n in (near, C - 1 - near, other):
                arrive(lig.at[n, k], li_in.at[n, k])
            cx[k] = cross_plain(k)
            right_of(k, cx[k])
        send_crt(B, c, 0, near)
        for h in range(2):
            arrive(test.at[h], ext_in.at[0, 3, h])
        for kk in range(KM):
            arrive(xr.at[kk], li_in.at[c, kk])
            cx[KN + kk] = xr[kk]
            right_of(KN + kk, xr[kk])
        for to in (other, C - 1 - near, near):
            send_crt(B, c, 1, to)

    core_part = None
    for k in range(K):
        weight = mask[0, 0, k].astype(F32) * scale
        hk, kk = (0, k) if k < KN else (1, k - KN)
        test_k = test[hk, :, kk * rank:(kk + 1) * rank]
        clt[k] = (mm(cx[k], test_k, (1, 1)) * weight).astype(BF16)
        term = mm(crt[c, :, k * rank:(k + 1) * rank], test_k, (1, 1))
        core_part = term if core_part is None else core_part + term
    cps[...] = core_part
    for o in range(1, D):
        send("cp", cps, cpr.at[d], cp_in.at[0], (r, c, lax.rem(d + o, D)), 0, 3)
    cpr[d] = core_part

    @pl.when(is_mid)
    def _():
        B = "mid"
        arrive(part_of(edge, 0), cr_in.at[edge, 0])
        send_crt(B, edge, 0, other)

    arrive(cpr.at[pl.ds(0, D - 1)], cp_in.at[0])
    core = cpr[0]
    for n in range(1, D):
        core = core + cpr[n]

    def relay_other(part):
        arrive(part_of(other, part), cr_in.at[other, part])
        send_crt("mid", other, part, edge)


    @pl.when(is_mid)
    def _():
        relay_other(0)

    gram = mm(core, core, (1, 1), HIGHEST)
    eye = (
        lax.broadcasted_iota(jnp.int32, (rank, rank), 0)
        == lax.broadcasted_iota(jnp.int32, (rank, rank), 1)
    ).astype(F32)
    trace = jnp.sum(core * core)
    ridge = 0.05 * trace / rank + 1e-05
    norm = 1.0 / jnp.broadcast_to(trace + ridge, (rank, rank))
    gram = (gram + ridge * eye) * norm
    start, scales = inverse_schedule(rank)
    rest = eye - start * gram
    inv = (scales[0] * start) * (eye + rest)
    rest = (1.0 - scales[0]) * eye + scales[0] * mm_split(rest, rest)
    for step, factor in enumerate(scales[1:]):
        if step == 5:

            @pl.when(is_mid)
            def _():
                send_crt("mid", c, 1, edge)

        both = mm_split(jnp.concatenate([inv, rest], axis=0), rest)
        inv = factor * (inv + both[:rank])
        rest = (1.0 - factor) * eye + factor * both[rank:]
    solved = mm_split(inv, core)
    solved = solved + mm_split(inv, core - mm(gram, solved, precision=HIGHEST))
    weights = (solved * (norm[:, 0:1] * rank**0.5)).astype(BF16)

    rows = KN * rank

    def zpart(n, part):
        return zz.at[n, pl.ds(0, rows) if part == 0 else pl.ds(rows, half)]

    def send_z(slot, part):
        send("all", zpart(r, part), zpart(r, part), z_in.at[slot, part], (across[slot], c, d),
             (KN if part == 0 else KM) * SQ)

    for part in range(2):
        for k in range(KN) if part == 0 else range(KN, K):
            zz[r, pl.ds(k * rank, rank)] = mm(clt[k], weights, (1, 1)).astype(BF16)
        send_z(part, part)
    for part in range(2):
        send_z(1 - part, part)

    @pl.when(is_mid)
    def _():
        B = "mid"
        far = C - 1 - edge
        relay_other(1)
        arrive(part_of(far, 0), cr_in.at[far, 0])
        send_crt(B, far, 0, edge)

    def relay_z(part, branch):
        via, to = (0, 1) if part == 0 else (1, 0)
        arrive(zpart(across[via], part), z_in.at[via, part])
        send(branch, zpart(across[via], part), zpart(across[via], part), z_in.at[2, part],
             (across[to], c, d), (KN if part == 0 else KM) * SQ)

    part_l = lo_h.shape[1] // D
    place = c * D + d
    owner, slot_l = place // C, lax.rem(place, C)

    def halves(left, right, contract, parts, got, sem, in_s, indices):
        size = left.shape[0] // D

        def keep(n, rows):
            for q, index in enumerate(indices):
                parts[n, index] = rows[:, q * rank:(q + 1) * rank]

        def share(n):
            for index in indices:
                send(sem[0], parts.at[n, index], got.at[index, d], in_s, (r, c, n), 0, sem[1])

        if D == 2:
            for n in (1 - d, d):
                keep(n, mm(left[pl.ds(pl.multiple_of(n * size, size), size), :], right, contract))
                if n is not d:
                    share(n)
        else:
            total = mm(left[...], right, contract)
            for n in range(D):
                keep(n, total[n * size:(n + 1) * size])
            for e in range(1, D):
                share(lax.rem(d + e, D))

    def range_mm(js, indices):
        right = jnp.concatenate([crt[j] for j in js], axis=0)
        halves(lo, right, (1, 1), rps, rpr, ("rp", 4), rp_in.at[indices[0] // 2], indices)

    def range_out(j, index, first, branch="all"):
        total = rps[d, index]
        if index % 2 == 0:
            arrive(rpr.at[pl.ds(index, 2), pl.ds(0, D - 1)], rp_in.at[index // 2])
        for e in range(1, D):
            total = total + rpr[index, lax.rem(d + e, D)]
        rsend[index] = total.astype(BF16)
        if first:
            @pl.when(owner != d)
            def _():
                send("ro", rsend.at[index], rout.at[slot_l], ro_in.at[0], (r, j, owner), part_l * rank * 2, 1)
        else:
            send(branch, rsend.at[index], rout.at[slot_l], ro_in.at[0], (r, j, owner), part_l * rank * 2)

    part_r = ro_h.shape[1] // D
    place_q = r * D + d
    owner_q, slot_q = place_q // R, lax.rem(place_q, R)

    def corange_mm(rows, indices):
        right = jnp.concatenate([zz[i] for i in rows], axis=1)
        halves(ro, right, (1, 0), qps, qpr, ("qp", 5), qp_in.at[(indices[0] + 1) // 2], indices)

    def corange_out(i, index, first):
        total = qps[d, index]
        if index != 2:
            arrive(qpr.at[pl.ds(index, 2 if index == 1 else 1), pl.ds(0, D - 1)], qp_in.at[(index + 1) // 2])
        for e in range(1, D):
            total = total + qpr[index, lax.rem(d + e, D)]
        qsend[index] = total.astype(BF16)
        if first:
            @pl.when(owner_q != d)
            def _():
                send("qo", qsend.at[index], qout.at[slot_q], qo_in.at[0], (i, c, owner_q), part_r * rank * 2, 2)
        else:
            send("all", qsend.at[index], qout.at[slot_q], qo_in.at[0], (i, c, owner_q), part_r * rank * 2)

    order = (c, jnp.where(is_end, near, other), jnp.where(is_end, C - 1 - near, C - 1 - edge),
             jnp.where(is_end, other, edge))

    corange_mm((r,), (0,))

    @pl.when(is_end)
    def _():
        for part in range(2):
            arrive(part_of(near, part), cr_in.at[near, part])

    range_mm(order[:2], (0, 1))

    @pl.when(is_end)
    def _():
        relay_z(0, "end")
        relay_z(1, "end")

    @pl.when(is_mid)
    def _():
        relay_z(0, "mid")
        relay_z(1, "mid")

    for index in range(2):
        range_out(order[index], index, index == 0)

    @pl.when(is_end)
    def _():
        for n in (C - 1 - near, other):
            for part in range(2):
                arrive(part_of(n, part), cr_in.at[n, part])

    @pl.when(is_mid)
    def _():
        for n in (C - 1 - edge, edge):
            arrive(part_of(n, 1), cr_in.at[n, 1])

    range_mm(order[2:], (2, 3))
    arrive(zpart(across[0], 1), z_in.at[0, 1])
    arrive(zpart(across[1], 0), z_in.at[1, 0])
    corange_mm(across[:2], (1, 2))
    range_out(order[2], 2, False)
    range_out(order[3], 3, False)
    corange_out(r, 0, True)
    for slot in range(2):
        corange_out(across[slot], slot + 1, False)
    for part in range(2):
        arrive(zpart(across[2], part), z_in.at[2, part])
    corange_mm(across[2:], (3,))
    corange_out(across[2], 3, False)

    @pl.when(owner == d)
    def _():
        rout[slot_l] = rsend[0]

    @pl.when(owner_q == d)
    def _():
        qout[slot_q] = qsend[0]

    def gather(out, rows, sem, owned):
        count = rows.shape[0]

        @pl.when(owned)
        def _():
            arrive(rows.at[pl.ds(0, count - 1)], sem.at[0])

        @pl.when(jnp.logical_not(owned))
        def _():
            arrive(rows, sem.at[0])

        size = rows.shape[1]
        for q in range(count):
            out[q * size:(q + 1) * size, :] = rows[q]

    gather(out_range, rout, ro_in, owner == d)
    gather(out_corange, qout, qo_in, owner_q == d)
    drain(3, cpr.at[pl.ds(0, D - 1)])
    drain(4, rpr.at[:, pl.ds(0, D - 1)])
    drain(5, qpr.at[:, pl.ds(0, D - 1)])
    for branch, cond in (("mid", is_mid), ("end", is_end)):
        @pl.when(cond)
        def _(branch=branch):
            drain(0, bytes_of(sent["all"] + sent[branch]))
    for branch, cond, sem in (("ro", owner != d, 1), ("qo", owner_q != d, 2)):
        @pl.when(cond)
        def _(branch=branch, sem=sem):
            drain(sem, bytes_of(sent[branch]))


def body(sizes, left_outer, left_inner, right_outer, right_inner, range_test, corange_test, product_mask):
    R, C, D = sizes
    K, BL, rank = left_outer.shape[1:]
    BR = right_outer.shape[2]
    sketch = corange_test.shape[2]
    assert R == 4 and C == 4 and K % R == 0 and BL == BR and BL % D == 0 and D > 1
    KM = K // 2
    KN = K - KM
    KQ = KN // 2
    KR = K // R
    dma = pltpu.SemaphoreType.DMA
    vmem = pltpu.VMEM
    scratch = [
        pltpu.SMEM((1, 1, K), jnp.int32),
        vmem((RULER, rank), BF16),
        vmem((BL, K * rank), BF16),
        vmem((BR, K * rank), BF16),
        vmem((K, BR, rank), BF16),
        vmem((BR, rank), BF16),
        vmem((BL, sketch), BF16),
        vmem((C, K, BL, rank), BF16),
        vmem((R, KN - KQ, rank, BR), BF16),
        vmem((R, KM, 2 * rank, BR), BF16),
        vmem((KQ, rank, BR), BF16),
        vmem((KM, rank, BR), BF16),
        vmem((sketch, K * rank), BF16),
        vmem((sketch, K * rank), BF16),
        vmem((sketch, KM * rank), BF16),
        vmem((sketch, KM * rank), BF16),
        vmem((2, sketch, KM * rank), BF16),
        vmem((sketch, KM * rank), F32),
        vmem((R, rank, KR * rank), F32),
        vmem((R - 1, rank, KR * rank), F32),
        vmem((R, rank, KR * rank), BF16),
        vmem((K, rank, rank), BF16),
        vmem((KM, rank, rank), BF16),
        vmem((KM, rank, rank), BF16),
        vmem((rank, sketch), F32),
        vmem((D, rank, sketch), F32),
        vmem((C, rank, K * rank), BF16),
        vmem((K, rank, sketch), BF16),
        vmem((R, K * rank, rank), BF16),
        vmem((D, C, BL // D, rank), F32),
        vmem((C, D, BL // D, rank), F32),
        vmem((C, BL // D, rank), BF16),
        vmem((C, BL // D, rank), BF16),
        vmem((D, R, BR // D, rank), F32),
        vmem((R, D, BR // D, rank), F32),
        vmem((R, BR // D, rank), BF16),
        vmem((R, BR // D, rank), BF16),
        dma((7,)), dma((6,)),
        dma((C, K)), dma((3, KN - KQ)), dma((2, 4, KM)), dma((1,)), dma((C, 2)), dma((3, 2)),
        dma((2,)), dma((1,)), dma((3,)), dma((1,)),
    ]
    whole = pl.BlockSpec(memory_space=pltpu.VMEM)
    out = jax.ShapeDtypeStruct((BL * C // D, rank), BF16)
    range_rows, corange_rows = pl.pallas_call(
        functools.partial(kernel, (R, C, D, K)),
        out_shape=(out, out),
        in_specs=[pl.BlockSpec(memory_space=pltpu.HBM)] * 7,
        out_specs=(whole, whole),
        scratch_shapes=scratch,
        compiler_params=pltpu.CompilerParams(
            collective_id=0, has_side_effects=True, vmem_limit_bytes=36 * 1024 * 1024
        ),
    )(*[
        pltpu.with_memory_space_constraint(x, pltpu.HBM)
        for x in (left_outer[0], left_inner[0], right_outer[0], right_inner[0],
                  range_test[0], corange_test[0], product_mask)
    ])
    return range_rows[None, None].astype(F32), corange_rows[None, None].astype(F32)


def solution(mesh):
    sizes = tuple(mesh.shape[name] for name in ("row", "col", "depth"))
    return jax.shard_map(
        functools.partial(body, sizes),
        mesh=mesh,
        in_specs=(
            P("row", "depth", "col", None),
            P("row", "depth", "col", None),
            P("col", "depth", "row", None),
            P("col", "depth", "row", None),
            P("col", "row", None),
            P("row", "col", None),
            P("row", "col", "depth"),
        ),
        out_specs=(P("row", "col", "depth", None), P("row", "col", "depth", None)),
        check_vma=False,
    )
```

```python
import functools

import jax
import jax.numpy as jnp
from jax import lax
from jax.experimental import pallas as pl
from jax.experimental.pallas import tpu as pltpu
from jax.sharding import PartitionSpec as P

F32 = jnp.float32
BF16 = jnp.bfloat16
HIGHEST = lax.Precision.HIGHEST
MESH = pl.DeviceIdType.MESH
RULER = 32768


def mm(a, b, contract=(1, 0), precision=None):
    dims = (((contract[0],), (contract[1],)), ((), ()))
    return lax.dot_general(a, b, dims, precision=precision, preferred_element_type=F32)


def mm_split(a, b):
    a_up, b_up = a.astype(BF16), b.astype(BF16)
    a_low, b_low = (a - a_up.astype(F32)).astype(BF16), (b - b_up.astype(F32)).astype(BF16)
    return mm(jnp.concatenate([a_up, a_up, a_low], axis=1), jnp.concatenate([b_up, b_low, b_up], axis=0))


def inverse_schedule(rank):
    low = 1.0 / (rank / 0.05 + 1.0)
    low *= 0.999
    start = 2.0 / (1.0 + low)
    err = 1.0 - low * start
    scales = []
    while err > 1e-3:
        scales.append(2.0 / (2.0 - err * err))
        err = err * err / (2.0 - err * err)
    return start, scales


def kernel(
    sizes,
    lo_h, li_h, ro_h, ri_h, rt_h, ct_h, mask_h,
    out_range, out_corange,
    mask, ruler, lo, ro, ri, rt, ct, lig, rig, rx, qx, ex, tp, tpe, tps, tpo, test, tmid, pps, ppr, probe,
    cx, xs, xr, cps, cpr, crt, clt, zz, rps, rpr, rsend, rout, qps, qpr, qsend, qout,
    load_s, send_s, li_in, ri_in, ext_in, cp_in, cr_in, z_in,
    rp_in, ro_in, qp_in, qo_in,
):
    R, C, D, K = sizes
    KM = K // 2
    KN = K - KM
    KQ = KN // 2
    KR = K // R
    rank = lo_h.shape[2]
    r, c, d = lax.axis_index("row"), lax.axis_index("col"), lax.axis_index("depth")
    is_end = jnp.logical_or(c == 0, c == C - 1)
    is_mid = jnp.logical_not(is_end)
    across = (r + 1 - 2 * lax.rem(r, 2), lax.rem(r + 2, R), R - 1 - r)
    sent = {}

    def send(branch, src, dst, recv, dev, size, sem=0):
        op = pltpu.make_async_remote_copy(
            src_ref=src, dst_ref=dst, send_sem=send_s.at[sem], recv_sem=recv,
            device_id=dev, device_id_type=MESH,
        )
        op.start()
        sent[branch] = sent.get(branch, 0) + size

    def arrive(ref, recv):
        pltpu.make_async_remote_copy(
            src_ref=ref, dst_ref=ref, send_sem=send_s.at[0], recv_sem=recv,
            device_id=(r, c, d), device_id_type=MESH,
        ).wait_recv()

    def drain(sem, ref):
        pltpu.make_async_remote_copy(
            src_ref=ref, dst_ref=ref, send_sem=send_s.at[sem], recv_sem=load_s.at[0],
            device_id=(r, c, d), device_id_type=MESH,
        ).wait_send()

    def bytes_of(size):
        return ruler.at[pl.ds(0, size // (2 * rank))]

    def load(src, dst, index):
        op = pltpu.make_async_copy(src, dst, load_s.at[index])
        op.start()
        return op

    bar = pltpu.get_barrier_semaphore()

    def greet(row, col, depth):
        pl.semaphore_signal(bar, inc=1, device_id=(row, col, depth), device_id_type=MESH)

    def greet_depth(row, col, own):
        if D <= 4:
            for e in range(1 if own else 0, D):
                greet(row, col, lax.rem(d + e, D))
        else:
            @pl.loop(1 if own else 0, D)
            def _(e):
                greet(row, col, lax.rem(d + e, D))

    greet_depth(r, c, True)
    for o in range(1, R):
        greet_depth(lax.rem(r + o, R), c, False)
    for o in range(1, C):
        greet_depth(r, lax.rem(c + o, C), False)
    load_ri = load(ri_h, ri, 0)
    load_ct = load(ct_h, ct, 1)
    for k in range(K):
        load(lo_h.at[k], lo.at[:, pl.ds(k * rank, rank)], 2)
    load_rt = load(rt_h, rt, 3)
    for k in range(K):
        load(ro_h.at[k], ro.at[:, pl.ds(k * rank, rank)], 4)
    load_li = load(li_h, lig.at[c], 5)
    load_mask = load(mask_h, mask, 6)

    pl.semaphore_wait(bar, R * D + C * D - D - 1)

    BLK = lig.shape[2] * rank * 2
    SQ = rank * rank * 2
    sketch = ct_h.shape[1]
    near = 1 + (c // (C - 1)) * (C - 3)
    edge = ((c - 1) // max(C - 3, 1)) * (C - 1)
    other = C - 1 - c
    half = KM * rank

    def send_li(branch, k, owner, dev, src=None):
        send(branch, lig.at[owner, k] if src is None else src, lig.at[owner, k],
             li_in.at[owner, k], dev, BLK)

    def send_ri(branch, k, owner, to, slot):
        send(branch, rig.at[owner, k - KQ], rig.at[owner, k - KQ], ri_in.at[slot, k - KQ], (to, c, d), BLK)

    def relay_ri(branch, k):
        via, to = (0, 1) if k % 2 == 0 else (1, 0)
        arrive(rig.at[across[via], k - KQ], ri_in.at[via, k - KQ])
        send_ri(branch, k, across[via], across[to], 2)

    def wait_ri(k, skip):
        for slot in range(3):
            if slot != skip:
                arrive(rig.at[across[slot], k - KQ], ri_in.at[slot, k - KQ])

    def via_of(k):
        return 0 if k % 2 == 0 else 1

    def tall(ref_row, kk, part):
        return rx.at[ref_row, kk, pl.ds(part * rank, rank)]

    def send_x(branch, kk, part, owner, to, slot):
        send(branch, tall(owner, kk, part), tall(owner, kk, part), ext_in.at[part, slot, kk],
             (to, c, d), BLK)

    def relay_x(branch, kk, part):
        via, to = (0, 1) if (kk + part) % 2 == 0 else (1, 0)
        arrive(tall(across[via], kk, part), ext_in.at[part, via, kk])
        send_x(branch, kk, part, across[via], across[to], 2)

    def wait_x(kk, part):
        for slot in range(3):
            if slot != (kk + part) % 2:
                arrive(tall(across[slot], kk, part), ext_in.at[part, slot, kk])

    def cross_tall(kk, k, to):
        total = None
        for b in range(C):
            term = mm(rx[b, kk], lig[b, k])
            total = term if total is None else total + term
        xs[kk] = total[rank:].astype(BF16)
        send("mid" if k >= KN else "end", xs.at[kk], xr.at[kk], li_in.at[to, kk], (r, to, d), SQ)
        cx[k] = total[:rank].astype(BF16)

    def tests():
        load_ct.wait()
        pltpu.make_async_copy(lo, lo, load_s.at[2]).wait()
        tp[...] = mm(ct[...].T, lo[...]).astype(BF16)

    def probes(branch):
        load_rt.wait()
        pltpu.make_async_copy(ro, ro, load_s.at[4]).wait()
        part = mm(rt[...].T, ro[...])
        for n in range(R):
            pps[n] = part[:, n * KR * rank:(n + 1) * KR * rank]
        for slot in range(3):
            send(branch, pps.at[across[slot]], ppr.at[slot], cr_in.at[c, 0],
                 (across[slot], c, d), KR * SQ * 2)

    def probe_sum(branch):
        arrive(ppr, cr_in.at[c, 0])
        total = pps[r]
        for slot in range(3):
            total = total + ppr[slot]
        probe[r] = total.astype(BF16)
        for slot in range(3):
            send(branch, probe.at[r], probe.at[r], cr_in.at[c, 1], (across[slot], c, d), KR * SQ)

    def probe_wait():
        arrive(probe.at[pl.ds(0, 3)], cr_in.at[c, 1])

    scale = (K * D) ** -0.5

    def cross_plain(k):
        total = None
        for b in range(C):
            term = mm(rig[b, k - KQ], lig[b, k])
            total = term if total is None else total + term
        return total.astype(BF16)

    def right_of(k, cross):
        weight = mask[0, 0, k].astype(F32) * scale
        lanes = pl.ds(k % KR * rank, rank)
        right = (mm(probe[k // KR, :, lanes], cross) * weight).astype(BF16)
        crt[c, :, pl.ds(k * rank, rank)] = right

    def fold(k):
        weight = mask[0, 0, k].astype(F32) * scale
        hk, kk = (0, k) if k < KN else (1, k - KN)
        test_k = test[hk, :, kk * rank:(kk + 1) * rank]
        clt[k] = (mm(cx[k], test_k, (1, 1)) * weight).astype(BF16)
        term = mm(crt[c, :, k * rank:(k + 1) * rank], test_k, (1, 1))
        cps[...] = term if k == 0 else cps[...] + term

    def part_of(n, part):
        return crt.at[n, :, pl.ds(0, KN * rank) if part == 0 else pl.ds(KN * rank, half)]

    def send_crt(branch, owner, part, to):
        send(branch, part_of(owner, part), part_of(owner, part), cr_in.at[owner, part],
             (r, to, d), (KN if part == 0 else KM) * SQ)

    @pl.when(is_mid)
    def _():
        B = "mid"
        for k in range(K):
            send_li(B, k, c, (r, other, d), li_h.at[k])
            if k < KN:
                send_li(B, k, c, (r, edge, d), li_h.at[k])
        load_ri.wait()
        for k in range(KQ):
            qx[k] = ri[k].T
            send(B, qx.at[k], tall(r, k, 1), ext_in.at[1, 3, k], (r, edge, d), BLK)
        for k in range(KQ, KN):
            rig[r, k - KQ] = ri[k].T
            for slot in range(2):
                send_ri(B, k, r, across[slot], slot)
        for kk in range(KM):
            rx[r, kk, 0:rank] = ri[KN + kk].T
            for slot in range(2):
                send_x(B, kk, 0, r, across[slot], slot)
        tests()
        probes(B)
        far = C - 1 - edge
        lower = c == 1
        h = jnp.where(lower, 0, 1)
        arrive(lig.at[edge, 0], li_in.at[edge, 0])
        send_li(B, 0, edge, (r, other, d))
        for k in range(KN):
            arrive(lig.at[other, k], li_in.at[other, k])
            send_li(B, k, other, (r, edge, d))
            if k >= KQ:
                relay_ri(B, k)
        relay_x(B, 0, 0)
        arrive(tpe, li_in.at[c, K - 2])
        both = tpe[...].astype(F32) + tp[...].astype(F32)
        tmid[...] = jnp.where(lower, both[:, 0:half], both[:, half:2 * half])
        tps[...] = jnp.where(lower, both[:, half:2 * half], both[:, 0:half]).astype(BF16)
        send(B, tps, tpo, li_in.at[other, K - 1], (r, other, d), sketch * half * 2)
        relay_x(B, 1, 0)
        for k in range(1, KN):
            arrive(lig.at[edge, k], li_in.at[edge, k])
            send_li(B, k, edge, (r, other, d))
        probe_sum(B)
        arrive(tall(r, 0, 1), ext_in.at[1, 3, 0])
        for slot in range(2):
            send_x(B, 0, 1, r, across[slot], slot)
        arrive(lig.at[far, 0], li_in.at[far, 0])
        send_li(B, 0, far, (r, edge, d))
        arrive(tpo, li_in.at[c, K - 1])
        test[h] = (tmid[...] + tpo[...].astype(F32)).astype(BF16)
        for to in (edge, other):
            send(B, test.at[h], test.at[h], ext_in.at[0, 3, h], (r, to, d), sketch * half * 2)
        arrive(tall(r, 1, 1), ext_in.at[1, 3, 1])
        for slot in range(2):
            send_x(B, 1, 1, r, across[slot], slot)
        arrive(lig.at[edge, KN], li_in.at[edge, KN])
        send_li(B, KN, edge, (r, other, d))
        for k in range(1, KN):
            arrive(lig.at[far, k], li_in.at[far, k])
            send_li(B, k, far, (r, edge, d))
        relay_x(B, 0, 1)
        for k in range(KN + 1, K):
            arrive(lig.at[edge, k], li_in.at[edge, k])
            send_li(B, k, edge, (r, other, d))
        arrive(test.at[1 - h], ext_in.at[0, 3, 1 - h])
        send(B, test.at[1 - h], test.at[1 - h], ext_in.at[0, 3, 1 - h], (r, edge, d), sketch * half * 2)
        for kk in range(1, KM):
            relay_x(B, kk, 1)
        for k in range(KQ, KN):
            wait_ri(k, via_of(k))
        load_li.wait()
        load_mask.wait()
        for k in range(KQ, KN):
            cx[k] = cross_plain(k)
        probe_wait()
        for k in range(KQ, KN):
            right_of(k, cx[k])
        for k in range(KQ):
            arrive(xr.at[k], li_in.at[c, k])
            cx[k] = xr[k]
            right_of(k, cx[k])
        send_crt(B, c, 0, other)
        send_crt(B, c, 0, edge)
        for k in range(KN):
            fold(k)
        for kk in range(KM):
            for part in range(2):
                wait_x(kk, part)
            for b in (other, far):
                arrive(lig.at[b, KN + kk], li_in.at[b, KN + kk])
            cross_tall(kk, KN + kk, edge)
            right_of(KN + kk, cx[KN + kk])
            if kk < KM - 1:
                fold(KN + kk)
        send_crt(B, c, 1, other)
        fold(K - 1)

    @pl.when(is_end)
    def _():
        B = "end"
        send_li(B, 0, c, (r, near, d), li_h.at[0])
        load_ri.wait()
        for k in range(KQ):
            rx[r, k, 0:rank] = ri[k].T
            for slot in range(2):
                send_x(B, k, 0, r, across[slot], slot)
        for k in range(KQ, KN):
            rig[r, k - KQ] = ri[k].T
            for slot in range(2):
                send_ri(B, k, r, across[slot], slot)
        tests()
        send(B, tp, tpe, li_in.at[near, K - 2], (r, near, d), sketch * K * rank * 2)
        for k in range(1, KN):
            send_li(B, k, c, (r, near, d), li_h.at[k])
        for kk in range(KM):
            ex[kk] = ri[KN + kk].T
            send(B, ex.at[kk], tall(r, kk, 1), ext_in.at[1, 3, kk], (r, near, d), BLK)
        for k in range(KN, K):
            send_li(B, k, c, (r, near, d), li_h.at[k])
        probes(B)
        for k in range(KQ):
            relay_x(B, k, 0)
        for k in range(KQ, KN):
            relay_ri(B, k)
        for k in range(KQ):
            arrive(tall(r, k, 1), ext_in.at[1, 3, k])
            for slot in range(2):
                send_x(B, k, 1, r, across[slot], slot)
        probe_sum(B)
        for k in range(KQ):
            relay_x(B, k, 1)
        load_li.wait()
        load_mask.wait()
        probe_wait()
        for k in range(KQ):
            for part in range(2):
                wait_x(k, part)
            for n in (near, C - 1 - near, other):
                arrive(lig.at[n, k], li_in.at[n, k])
            cross_tall(k, k, near)
            right_of(k, cx[k])
        for k in range(KQ, KN):
            wait_ri(k, via_of(k))
            for n in (near, C - 1 - near, other):
                arrive(lig.at[n, k], li_in.at[n, k])
            cx[k] = cross_plain(k)
            right_of(k, cx[k])
        send_crt(B, c, 0, near)
        for h in range(2):
            arrive(test.at[h], ext_in.at[0, 3, h])
        for k in range(KN):
            fold(k)
        for kk in range(KM):
            arrive(xr.at[kk], li_in.at[c, kk])
            cx[KN + kk] = xr[kk]
            right_of(KN + kk, xr[kk])
            fold(KN + kk)
        for to in (other, C - 1 - near, near):
            send_crt(B, c, 1, to)

    for o in range(1, D):
        send("cp", cps, cpr.at[d], cp_in.at[0], (r, c, lax.rem(d + o, D)), 0, 3)
    cpr[d] = cps[...]

    @pl.when(is_mid)
    def _():
        B = "mid"
        arrive(part_of(edge, 0), cr_in.at[edge, 0])
        send_crt(B, edge, 0, other)

    arrive(cpr.at[pl.ds(0, D - 1)], cp_in.at[0])
    core = cpr[0]
    for n in range(1, D):
        core = core + cpr[n]

    def relay_other(part):
        arrive(part_of(other, part), cr_in.at[other, part])
        send_crt("mid", other, part, edge)


    @pl.when(is_mid)
    def _():
        relay_other(0)

    gram = mm(core, core, (1, 1), HIGHEST)
    eye = (
        lax.broadcasted_iota(jnp.int32, (rank, rank), 0)
        == lax.broadcasted_iota(jnp.int32, (rank, rank), 1)
    ).astype(F32)
    trace = jnp.sum(core * core)
    ridge = 0.05 * trace / rank + 1e-05
    norm = 1.0 / jnp.broadcast_to(trace + ridge, (rank, rank))
    gram = (gram + ridge * eye) * norm
    start, scales = inverse_schedule(rank)
    rest = eye - start * gram
    inv = (scales[0] * start) * (eye + rest)
    rest = (1.0 - scales[0]) * eye + scales[0] * mm_split(rest, rest)
    for step, factor in enumerate(scales[1:]):
        if step == 5:

            @pl.when(is_mid)
            def _():
                send_crt("mid", c, 1, edge)

        both = mm_split(jnp.concatenate([inv, rest], axis=0), rest)
        inv = factor * (inv + both[:rank])
        rest = (1.0 - factor) * eye + factor * both[rank:]
    solved = mm_split(inv, core)
    solved = solved + mm_split(inv, core - mm(gram, solved, precision=HIGHEST))
    weights = (solved * (norm[:, 0:1] * rank**0.5)).astype(BF16)

    rows = KN * rank

    def zpart(n, part):
        return zz.at[n, pl.ds(0, rows) if part == 0 else pl.ds(rows, half)]

    def send_z(slot, part):
        send("all", zpart(r, part), zpart(r, part), z_in.at[slot, part], (across[slot], c, d),
             (KN if part == 0 else KM) * SQ)

    for part in range(2):
        for k in range(KN) if part == 0 else range(KN, K):
            zz[r, pl.ds(k * rank, rank)] = mm(clt[k], weights, (1, 1)).astype(BF16)
        send_z(part, part)
    for part in range(2):
        send_z(1 - part, part)

    @pl.when(is_mid)
    def _():
        B = "mid"
        far = C - 1 - edge
        relay_other(1)
        arrive(part_of(far, 0), cr_in.at[far, 0])
        send_crt(B, far, 0, edge)

    def relay_z(part, branch):
        via, to = (0, 1) if part == 0 else (1, 0)
        arrive(zpart(across[via], part), z_in.at[via, part])
        send(branch, zpart(across[via], part), zpart(across[via], part), z_in.at[2, part],
             (across[to], c, d), (KN if part == 0 else KM) * SQ)

    part_l = lo_h.shape[1] // D
    place = c * D + d
    owner, slot_l = place // C, lax.rem(place, C)

    def halves(left, right, contract, parts, got, sem, in_s, indices):
        size = left.shape[0] // D

        def keep(n, rows):
            for q, index in enumerate(indices):
                parts[n, index] = rows[:, q * rank:(q + 1) * rank]

        def share(n):
            for index in indices:
                send(sem[0], parts.at[n, index], got.at[index, d], in_s, (r, c, n), 0, sem[1])

        if D == 2:
            for n in (1 - d, d):
                keep(n, mm(left[pl.ds(pl.multiple_of(n * size, size), size), :], right, contract))
                if n is not d:
                    share(n)
        else:
            total = mm(left[...], right, contract)
            for n in range(D):
                keep(n, total[n * size:(n + 1) * size])
            for e in range(1, D):
                share(lax.rem(d + e, D))

    def range_mm(js, indices):
        right = jnp.concatenate([crt[j] for j in js], axis=0)
        halves(lo, right, (1, 1), rps, rpr, ("rp", 4), rp_in.at[indices[0] // 2], indices)

    def range_out(j, index, first, branch="all"):
        total = rps[d, index]
        if index % 2 == 0:
            arrive(rpr.at[pl.ds(index, 2), pl.ds(0, D - 1)], rp_in.at[index // 2])
        for e in range(1, D):
            total = total + rpr[index, lax.rem(d + e, D)]
        rsend[index] = total.astype(BF16)
        if first:
            @pl.when(owner != d)
            def _():
                send("ro", rsend.at[index], rout.at[slot_l], ro_in.at[0], (r, j, owner), part_l * rank * 2, 1)
        else:
            send(branch, rsend.at[index], rout.at[slot_l], ro_in.at[0], (r, j, owner), part_l * rank * 2)

    part_r = ro_h.shape[1] // D
    place_q = r * D + d
    owner_q, slot_q = place_q // R, lax.rem(place_q, R)

    def corange_mm(rows, indices):
        right = jnp.concatenate([zz[i] for i in rows], axis=1)
        halves(ro, right, (1, 0), qps, qpr, ("qp", 5), qp_in.at[(indices[0] + 1) // 2], indices)

    def corange_out(i, index, first):
        total = qps[d, index]
        if index != 2:
            arrive(qpr.at[pl.ds(index, 2 if index == 1 else 1), pl.ds(0, D - 1)], qp_in.at[(index + 1) // 2])
        for e in range(1, D):
            total = total + qpr[index, lax.rem(d + e, D)]
        qsend[index] = total.astype(BF16)
        if first:
            @pl.when(owner_q != d)
            def _():
                send("qo", qsend.at[index], qout.at[slot_q], qo_in.at[0], (i, c, owner_q), part_r * rank * 2, 2)
        else:
            send("all", qsend.at[index], qout.at[slot_q], qo_in.at[0], (i, c, owner_q), part_r * rank * 2)

    order = (c, jnp.where(is_end, near, other), jnp.where(is_end, C - 1 - near, C - 1 - edge),
             jnp.where(is_end, other, edge))

    corange_mm((r,), (0,))

    @pl.when(is_end)
    def _():
        for part in range(2):
            arrive(part_of(near, part), cr_in.at[near, part])

    range_mm(order[:2], (0, 1))

    @pl.when(is_end)
    def _():
        relay_z(0, "end")
        relay_z(1, "end")

    @pl.when(is_mid)
    def _():
        relay_z(0, "mid")
        relay_z(1, "mid")

    for index in range(2):
        range_out(order[index], index, index == 0)

    @pl.when(is_end)
    def _():
        for n in (C - 1 - near, other):
            for part in range(2):
                arrive(part_of(n, part), cr_in.at[n, part])

    @pl.when(is_mid)
    def _():
        for n in (C - 1 - edge, edge):
            arrive(part_of(n, 1), cr_in.at[n, 1])

    range_mm(order[2:], (2, 3))
    arrive(zpart(across[0], 1), z_in.at[0, 1])
    arrive(zpart(across[1], 0), z_in.at[1, 0])
    corange_mm(across[:2], (1, 2))
    range_out(order[2], 2, False)
    range_out(order[3], 3, False)
    corange_out(r, 0, True)
    for slot in range(2):
        corange_out(across[slot], slot + 1, False)
    for part in range(2):
        arrive(zpart(across[2], part), z_in.at[2, part])
    corange_mm(across[2:], (3,))
    corange_out(across[2], 3, False)

    @pl.when(owner == d)
    def _():
        rout[slot_l] = rsend[0]

    @pl.when(owner_q == d)
    def _():
        qout[slot_q] = qsend[0]

    def gather(out, rows, sem, owned):
        count = rows.shape[0]

        @pl.when(owned)
        def _():
            arrive(rows.at[pl.ds(0, count - 1)], sem.at[0])

        @pl.when(jnp.logical_not(owned))
        def _():
            arrive(rows, sem.at[0])

        size = rows.shape[1]
        for q in range(count):
            out[q * size:(q + 1) * size, :] = rows[q]

    gather(out_range, rout, ro_in, owner == d)
    gather(out_corange, qout, qo_in, owner_q == d)
    drain(3, cpr.at[pl.ds(0, D - 1)])
    drain(4, rpr.at[:, pl.ds(0, D - 1)])
    drain(5, qpr.at[:, pl.ds(0, D - 1)])
    for branch, cond in (("mid", is_mid), ("end", is_end)):
        @pl.when(cond)
        def _(branch=branch):
            drain(0, bytes_of(sent["all"] + sent[branch]))
    for branch, cond, sem in (("ro", owner != d, 1), ("qo", owner_q != d, 2)):
        @pl.when(cond)
        def _(branch=branch, sem=sem):
            drain(sem, bytes_of(sent[branch]))


def body(sizes, left_outer, left_inner, right_outer, right_inner, range_test, corange_test, product_mask):
    R, C, D = sizes
    K, BL, rank = left_outer.shape[1:]
    BR = right_outer.shape[2]
    sketch = corange_test.shape[2]
    assert R == 4 and C == 4 and K % R == 0 and BL == BR and BL % D == 0 and D > 1
    KM = K // 2
    KN = K - KM
    KQ = KN // 2
    KR = K // R
    dma = pltpu.SemaphoreType.DMA
    vmem = pltpu.VMEM
    scratch = [
        pltpu.SMEM((1, 1, K), jnp.int32),
        vmem((RULER, rank), BF16),
        vmem((BL, K * rank), BF16),
        vmem((BR, K * rank), BF16),
        vmem((K, BR, rank), BF16),
        vmem((BR, rank), BF16),
        vmem((BL, sketch), BF16),
        vmem((C, K, BL, rank), BF16),
        vmem((R, KN - KQ, rank, BR), BF16),
        vmem((R, KM, 2 * rank, BR), BF16),
        vmem((KQ, rank, BR), BF16),
        vmem((KM, rank, BR), BF16),
        vmem((sketch, K * rank), BF16),
        vmem((sketch, K * rank), BF16),
        vmem((sketch, KM * rank), BF16),
        vmem((sketch, KM * rank), BF16),
        vmem((2, sketch, KM * rank), BF16),
        vmem((sketch, KM * rank), F32),
        vmem((R, rank, KR * rank), F32),
        vmem((R - 1, rank, KR * rank), F32),
        vmem((R, rank, KR * rank), BF16),
        vmem((K, rank, rank), BF16),
        vmem((KM, rank, rank), BF16),
        vmem((KM, rank, rank), BF16),
        vmem((rank, sketch), F32),
        vmem((D, rank, sketch), F32),
        vmem((C, rank, K * rank), BF16),
        vmem((K, rank, sketch), BF16),
        vmem((R, K * rank, rank), BF16),
        vmem((D, C, BL // D, rank), F32),
        vmem((C, D, BL // D, rank), F32),
        vmem((C, BL // D, rank), BF16),
        vmem((C, BL // D, rank), BF16),
        vmem((D, R, BR // D, rank), F32),
        vmem((R, D, BR // D, rank), F32),
        vmem((R, BR // D, rank), BF16),
        vmem((R, BR // D, rank), BF16),
        dma((7,)), dma((6,)),
        dma((C, K)), dma((3, KN - KQ)), dma((2, 4, KM)), dma((1,)), dma((C, 2)), dma((3, 2)),
        dma((2,)), dma((1,)), dma((3,)), dma((1,)),
    ]
    whole = pl.BlockSpec(memory_space=pltpu.VMEM)
    out = jax.ShapeDtypeStruct((BL * C // D, rank), BF16)
    range_rows, corange_rows = pl.pallas_call(
        functools.partial(kernel, (R, C, D, K)),
        out_shape=(out, out),
        in_specs=[pl.BlockSpec(memory_space=pltpu.HBM)] * 7,
        out_specs=(whole, whole),
        scratch_shapes=scratch,
        compiler_params=pltpu.CompilerParams(
            collective_id=0, has_side_effects=True, vmem_limit_bytes=36 * 1024 * 1024
        ),
    )(*[
        pltpu.with_memory_space_constraint(x, pltpu.HBM)
        for x in (left_outer[0], left_inner[0], right_outer[0], right_inner[0],
                  range_test[0], corange_test[0], product_mask)
    ])
    return range_rows[None, None].astype(F32), corange_rows[None, None].astype(F32)


def solution(mesh):
    sizes = tuple(mesh.shape[name] for name in ("row", "col", "depth"))
    return jax.shard_map(
        functools.partial(body, sizes),
        mesh=mesh,
        in_specs=(
            P("row", "depth", "col", None),
            P("row", "depth", "col", None),
            P("col", "depth", "row", None),
            P("col", "depth", "row", None),
            P("col", "row", None),
            P("row", "col", None),
            P("row", "col", "depth"),
        ),
        out_specs=(P("row", "col", "depth", None), P("row", "col", "depth", None)),
        check_vma=False,
    )
```

```python
import functools

import jax
import jax.numpy as jnp
from jax import lax
from jax.experimental import pallas as pl
from jax.experimental.pallas import tpu as pltpu
from jax.sharding import PartitionSpec as P

F32 = jnp.float32
BF16 = jnp.bfloat16
HIGHEST = lax.Precision.HIGHEST
MESH = pl.DeviceIdType.MESH
RULER = 32768


def mm(a, b, contract=(1, 0), precision=None):
    dims = (((contract[0],), (contract[1],)), ((), ()))
    return lax.dot_general(a, b, dims, precision=precision, preferred_element_type=F32)


def mm_split(a, b):
    a_up, b_up = a.astype(BF16), b.astype(BF16)
    a_low, b_low = (a - a_up.astype(F32)).astype(BF16), (b - b_up.astype(F32)).astype(BF16)
    return mm(jnp.concatenate([a_up, a_up, a_low], axis=1), jnp.concatenate([b_up, b_low, b_up], axis=0))


def inverse_schedule(rank):
    low = 1.0 / (rank / 0.05 + 1.0)
    low *= 0.999
    start = 2.0 / (1.0 + low)
    err = 1.0 - low * start
    scales = []
    while err > 1e-3:
        scales.append(2.0 / (2.0 - err * err))
        err = err * err / (2.0 - err * err)
    return start, scales


def kernel(
    sizes,
    lo_h, li_h, ro_h, ri_h, rt_h, ct_h, mask_h,
    out_range, out_corange,
    mask, ruler, lo, ro, ri, rt, ct, lig, rig, rx, qx, ex, tp, tpe, tps, tpo, test, tmid, pps, ppr, probe,
    cx, xs, xr, cps, cpr, crt, clt, zz, rps, rpr, rsend, rout, qps, qpr, qsend, qout,
    load_s, send_s, li_in, ri_in, ext_in, half_in, cp_in, cr_in, z_in,
    rp_in, ro_in, qp_in, qo_in,
):
    R, C, D, K = sizes
    KM = K // 2
    KN = K - KM
    KQ = KN // 2
    KR = K // R
    rank = lo_h.shape[2]
    r, c, d = lax.axis_index("row"), lax.axis_index("col"), lax.axis_index("depth")
    is_end = jnp.logical_or(c == 0, c == C - 1)
    is_mid = jnp.logical_not(is_end)
    across = (r + 1 - 2 * lax.rem(r, 2), lax.rem(r + 2, R), R - 1 - r)
    sent = {}

    def send(branch, src, dst, recv, dev, size, sem=0):
        op = pltpu.make_async_remote_copy(
            src_ref=src, dst_ref=dst, send_sem=send_s.at[sem], recv_sem=recv,
            device_id=dev, device_id_type=MESH,
        )
        op.start()
        sent[branch] = sent.get(branch, 0) + size

    def arrive(ref, recv):
        pltpu.make_async_remote_copy(
            src_ref=ref, dst_ref=ref, send_sem=send_s.at[0], recv_sem=recv,
            device_id=(r, c, d), device_id_type=MESH,
        ).wait_recv()

    def drain(sem, ref):
        pltpu.make_async_remote_copy(
            src_ref=ref, dst_ref=ref, send_sem=send_s.at[sem], recv_sem=load_s.at[0],
            device_id=(r, c, d), device_id_type=MESH,
        ).wait_send()

    def bytes_of(size):
        return ruler.at[pl.ds(0, size // (2 * rank))]

    def load(src, dst, index):
        op = pltpu.make_async_copy(src, dst, load_s.at[index])
        op.start()
        return op

    bar = pltpu.get_barrier_semaphore()

    def greet(row, col, depth):
        pl.semaphore_signal(bar, inc=1, device_id=(row, col, depth), device_id_type=MESH)

    def greet_depth(row, col, own):
        if D <= 4:
            for e in range(1 if own else 0, D):
                greet(row, col, lax.rem(d + e, D))
        else:
            @pl.loop(1 if own else 0, D)
            def _(e):
                greet(row, col, lax.rem(d + e, D))

    greet_depth(r, c, True)
    for o in range(1, R):
        greet_depth(lax.rem(r + o, R), c, False)
    for o in range(1, C):
        greet_depth(r, lax.rem(c + o, C), False)
    load_ri = load(ri_h, ri, 0)
    load_ct = load(ct_h, ct, 1)
    for k in range(K):
        load(lo_h.at[k], lo.at[:, pl.ds(k * rank, rank)], 2)
    load_rt = load(rt_h, rt, 3)
    for k in range(K):
        load(ro_h.at[k], ro.at[:, pl.ds(k * rank, rank)], 4)
    load_li = load(li_h, lig.at[c], 5)
    load_mask = load(mask_h, mask, 6)

    pl.semaphore_wait(bar, R * D + C * D - D - 1)

    BLK = lig.shape[2] * rank * 2
    SQ = rank * rank * 2
    sketch = ct_h.shape[1]
    near = 1 + (c // (C - 1)) * (C - 3)
    edge = ((c - 1) // max(C - 3, 1)) * (C - 1)
    other = C - 1 - c
    half = KM * rank

    def send_li(branch, k, owner, dev, src=None):
        send(branch, lig.at[owner, k] if src is None else src, lig.at[owner, k],
             li_in.at[owner, k], dev, BLK)

    def send_ri(branch, k, owner, to, slot):
        send(branch, rig.at[owner, k - KQ], rig.at[owner, k - KQ], ri_in.at[slot, k - KQ], (to, c, d), BLK)

    def relay_ri(branch, k):
        via, to = (0, 1) if k % 2 == 0 else (1, 0)
        arrive(rig.at[across[via], k - KQ], ri_in.at[via, k - KQ])
        send_ri(branch, k, across[via], across[to], 2)

    def wait_ri(k, skip):
        for slot in range(3):
            if slot != skip:
                arrive(rig.at[across[slot], k - KQ], ri_in.at[slot, k - KQ])

    def via_of(k):
        return 0 if k % 2 == 0 else 1

    def tall(ref_row, kk, part):
        return rx.at[ref_row, kk, pl.ds(part * rank, rank)]

    def pieces(branch, owner, kk, part, slot):
        if branch == "mid" and part == 1 and kk == KM - 1:
            size = rank // 2
            return [(rx.at[owner, kk, pl.ds(part * rank + q * size, size)], half_in.at[slot, q]) for q in range(2)]
        return [(tall(owner, kk, part), ext_in.at[part, slot, kk])]

    def send_x(branch, kk, part, owner, to, slot):
        parts = pieces(branch, owner, kk, part, slot)
        for ref, sem in parts:
            send(branch, ref, ref, sem, (to, c, d), BLK // len(parts))

    def relay_x(branch, kk, part):
        via, to = (0, 1) if (kk + part) % 2 == 0 else (1, 0)
        got = pieces(branch, across[via], kk, part, via)
        left = pieces(branch, across[via], kk, part, 2)
        for (ref, sem), (_, out) in zip(got, left):
            arrive(ref, sem)
            send(branch, ref, ref, out, (across[to], c, d), BLK // len(got))

    def wait_x(branch, kk, part):
        for slot in range(3):
            if slot != (kk + part) % 2:
                for ref, sem in pieces(branch, across[slot], kk, part, slot):
                    arrive(ref, sem)

    def cross_tall(kk, k, to):
        total = None
        for b in range(C):
            term = mm(rx[b, kk], lig[b, k])
            total = term if total is None else total + term
        xs[kk] = total[rank:].astype(BF16)
        send("mid" if k >= KN else "end", xs.at[kk], xr.at[kk], li_in.at[to, kk], (r, to, d), SQ)
        cx[k] = total[:rank].astype(BF16)

    def tests():
        load_ct.wait()
        pltpu.make_async_copy(lo, lo, load_s.at[2]).wait()
        tp[...] = mm(ct[...].T, lo[...]).astype(BF16)

    def probes(branch):
        load_rt.wait()
        pltpu.make_async_copy(ro, ro, load_s.at[4]).wait()
        part = mm(rt[...].T, ro[...])
        for n in range(R):
            pps[n] = part[:, n * KR * rank:(n + 1) * KR * rank]
        for slot in range(3):
            send(branch, pps.at[across[slot]], ppr.at[slot], cr_in.at[c, 0],
                 (across[slot], c, d), KR * SQ * 2)

    def probe_sum(branch):
        arrive(ppr, cr_in.at[c, 0])
        total = pps[r]
        for slot in range(3):
            total = total + ppr[slot]
        probe[r] = total.astype(BF16)
        for slot in range(3):
            send(branch, probe.at[r], probe.at[r], cr_in.at[c, 1], (across[slot], c, d), KR * SQ)

    def probe_wait():
        arrive(probe.at[pl.ds(0, 3)], cr_in.at[c, 1])

    scale = (K * D) ** -0.5

    def cross_plain(k):
        total = None
        for b in range(C):
            term = mm(rig[b, k - KQ], lig[b, k])
            total = term if total is None else total + term
        return total.astype(BF16)

    def right_of(k, cross):
        weight = mask[0, 0, k].astype(F32) * scale
        lanes = pl.ds(k % KR * rank, rank)
        right = (mm(probe[k // KR, :, lanes], cross) * weight).astype(BF16)
        crt[c, :, pl.ds(k * rank, rank)] = right

    def part_of(n, part):
        return crt.at[n, :, pl.ds(0, KN * rank) if part == 0 else pl.ds(KN * rank, half)]

    def send_crt(branch, owner, part, to):
        send(branch, part_of(owner, part), part_of(owner, part), cr_in.at[owner, part],
             (r, to, d), (KN if part == 0 else KM) * SQ)

    @pl.when(is_mid)
    def _():
        B = "mid"
        for k in range(K):
            send_li(B, k, c, (r, other, d), li_h.at[k])
            if k < KN:
                send_li(B, k, c, (r, edge, d), li_h.at[k])
        load_ri.wait()
        for k in range(KQ):
            qx[k] = ri[k].T
            send(B, qx.at[k], tall(r, k, 1), ext_in.at[1, 3, k], (r, edge, d), BLK)
        for k in range(KQ, KN):
            rig[r, k - KQ] = ri[k].T
            for slot in range(2):
                send_ri(B, k, r, across[slot], slot)
        for kk in range(KM):
            rx[r, kk, 0:rank] = ri[KN + kk].T
            for slot in range(2):
                send_x(B, kk, 0, r, across[slot], slot)
        tests()
        probes(B)
        far = C - 1 - edge
        lower = c == 1
        h = jnp.where(lower, 0, 1)
        arrive(lig.at[edge, 0], li_in.at[edge, 0])
        send_li(B, 0, edge, (r, other, d))
        for k in range(KN):
            arrive(lig.at[other, k], li_in.at[other, k])
            send_li(B, k, other, (r, edge, d))
            if k >= KQ:
                relay_ri(B, k)
        relay_x(B, 0, 0)
        arrive(tpe, li_in.at[c, K - 2])
        both = tpe[...].astype(F32) + tp[...].astype(F32)
        tmid[...] = jnp.where(lower, both[:, 0:half], both[:, half:2 * half])
        tps[...] = jnp.where(lower, both[:, half:2 * half], both[:, 0:half]).astype(BF16)
        send(B, tps, tpo, li_in.at[other, K - 1], (r, other, d), sketch * half * 2)
        relay_x(B, 1, 0)
        for k in range(1, KN):
            arrive(lig.at[edge, k], li_in.at[edge, k])
            send_li(B, k, edge, (r, other, d))
        probe_sum(B)
        arrive(tall(r, 0, 1), ext_in.at[1, 3, 0])
        for slot in range(2):
            send_x(B, 0, 1, r, across[slot], slot)
        arrive(lig.at[far, 0], li_in.at[far, 0])
        send_li(B, 0, far, (r, edge, d))
        arrive(tpo, li_in.at[c, K - 1])
        test[h] = (tmid[...] + tpo[...].astype(F32)).astype(BF16)
        for to in (edge, other):
            send(B, test.at[h], test.at[h], ext_in.at[0, 3, h], (r, to, d), sketch * half * 2)
        arrive(tall(r, 1, 1), ext_in.at[1, 3, 1])
        for slot in range(2):
            send_x(B, 1, 1, r, across[slot], slot)
        arrive(lig.at[edge, KN], li_in.at[edge, KN])
        send_li(B, KN, edge, (r, other, d))
        for k in range(1, KN):
            arrive(lig.at[far, k], li_in.at[far, k])
            send_li(B, k, far, (r, edge, d))
        relay_x(B, 0, 1)
        for k in range(KN + 1, K):
            arrive(lig.at[edge, k], li_in.at[edge, k])
            send_li(B, k, edge, (r, other, d))
        arrive(test.at[1 - h], ext_in.at[0, 3, 1 - h])
        send(B, test.at[1 - h], test.at[1 - h], ext_in.at[0, 3, 1 - h], (r, edge, d), sketch * half * 2)
        for kk in range(1, KM):
            relay_x(B, kk, 1)
        for k in range(KQ, KN):
            wait_ri(k, via_of(k))
        load_li.wait()
        load_mask.wait()
        for k in range(KQ, KN):
            cx[k] = cross_plain(k)
        probe_wait()
        for k in range(KQ, KN):
            right_of(k, cx[k])
        for k in range(KQ):
            arrive(xr.at[k], li_in.at[c, k])
            cx[k] = xr[k]
            right_of(k, cx[k])
        send_crt(B, c, 0, other)
        send_crt(B, c, 0, edge)
        for kk in range(KM):
            for part in range(2):
                wait_x(B, kk, part)
            for b in (other, far):
                arrive(lig.at[b, KN + kk], li_in.at[b, KN + kk])
            cross_tall(kk, KN + kk, edge)
        for k in range(KN, K):
            right_of(k, cx[k])
        send_crt(B, c, 1, other)

    @pl.when(is_end)
    def _():
        B = "end"
        send_li(B, 0, c, (r, near, d), li_h.at[0])
        load_ri.wait()
        for k in range(KQ):
            rx[r, k, 0:rank] = ri[k].T
            for slot in range(2):
                send_x(B, k, 0, r, across[slot], slot)
        for k in range(KQ, KN):
            rig[r, k - KQ] = ri[k].T
            for slot in range(2):
                send_ri(B, k, r, across[slot], slot)
        tests()
        send(B, tp, tpe, li_in.at[near, K - 2], (r, near, d), sketch * K * rank * 2)
        for k in range(1, KN):
            send_li(B, k, c, (r, near, d), li_h.at[k])
        for kk in range(KM):
            ex[kk] = ri[KN + kk].T
            send(B, ex.at[kk], tall(r, kk, 1), ext_in.at[1, 3, kk], (r, near, d), BLK)
        for k in range(KN, K):
            send_li(B, k, c, (r, near, d), li_h.at[k])
        probes(B)
        for k in range(KQ):
            relay_x(B, k, 0)
        for k in range(KQ, KN):
            relay_ri(B, k)
        for k in range(KQ):
            arrive(tall(r, k, 1), ext_in.at[1, 3, k])
            for slot in range(2):
                send_x(B, k, 1, r, across[slot], slot)
        probe_sum(B)
        for k in range(KQ):
            relay_x(B, k, 1)
        load_li.wait()
        load_mask.wait()
        probe_wait()
        for k in range(KQ):
            for part in range(2):
                wait_x(B, k, part)
            for n in (near, C - 1 - near, other):
                arrive(lig.at[n, k], li_in.at[n, k])
            cross_tall(k, k, near)
            right_of(k, cx[k])
        for k in range(KQ, KN):
            wait_ri(k, via_of(k))
            for n in (near, C - 1 - near, other):
                arrive(lig.at[n, k], li_in.at[n, k])
            cx[k] = cross_plain(k)
            right_of(k, cx[k])
        send_crt(B, c, 0, near)
        for h in range(2):
            arrive(test.at[h], ext_in.at[0, 3, h])
        for kk in range(KM):
            arrive(xr.at[kk], li_in.at[c, kk])
            cx[KN + kk] = xr[kk]
            right_of(KN + kk, xr[kk])
        for to in (other, C - 1 - near, near):
            send_crt(B, c, 1, to)

    core_part = None
    for k in range(K):
        weight = mask[0, 0, k].astype(F32) * scale
        hk, kk = (0, k) if k < KN else (1, k - KN)
        test_k = test[hk, :, kk * rank:(kk + 1) * rank]
        clt[k] = (mm(cx[k], test_k, (1, 1)) * weight).astype(BF16)
        term = mm(crt[c, :, k * rank:(k + 1) * rank], test_k, (1, 1))
        core_part = term if core_part is None else core_part + term
    cps[...] = core_part
    for o in range(1, D):
        send("cp", cps, cpr.at[d], cp_in.at[0], (r, c, lax.rem(d + o, D)), 0, 3)
    cpr[d] = core_part

    @pl.when(is_mid)
    def _():
        B = "mid"
        arrive(part_of(edge, 0), cr_in.at[edge, 0])
        send_crt(B, edge, 0, other)

    arrive(cpr.at[pl.ds(0, D - 1)], cp_in.at[0])
    core = cpr[0]
    for n in range(1, D):
        core = core + cpr[n]

    def relay_other(part):
        arrive(part_of(other, part), cr_in.at[other, part])
        send_crt("mid", other, part, edge)


    @pl.when(is_mid)
    def _():
        relay_other(0)

    gram = mm(core, core, (1, 1), HIGHEST)
    eye = (
        lax.broadcasted_iota(jnp.int32, (rank, rank), 0)
        == lax.broadcasted_iota(jnp.int32, (rank, rank), 1)
    ).astype(F32)
    trace = jnp.sum(core * core)
    ridge = 0.05 * trace / rank + 1e-05
    norm = 1.0 / jnp.broadcast_to(trace + ridge, (rank, rank))
    gram = (gram + ridge * eye) * norm
    start, scales = inverse_schedule(rank)
    rest = eye - start * gram
    inv = (scales[0] * start) * (eye + rest)
    rest = (1.0 - scales[0]) * eye + scales[0] * mm_split(rest, rest)
    for step, factor in enumerate(scales[1:]):
        if step == 5:

            @pl.when(is_mid)
            def _():
                send_crt("mid", c, 1, edge)

        both = mm_split(jnp.concatenate([inv, rest], axis=0), rest)
        inv = factor * (inv + both[:rank])
        rest = (1.0 - factor) * eye + factor * both[rank:]
    solved = mm_split(inv, core)
    solved = solved + mm_split(inv, core - mm(gram, solved, precision=HIGHEST))
    weights = (solved * (norm[:, 0:1] * rank**0.5)).astype(BF16)

    rows = KN * rank

    def zpart(n, part):
        return zz.at[n, pl.ds(0, rows) if part == 0 else pl.ds(rows, half)]

    def send_z(slot, part):
        send("all", zpart(r, part), zpart(r, part), z_in.at[slot, part], (across[slot], c, d),
             (KN if part == 0 else KM) * SQ)

    for part in range(2):
        for k in range(KN) if part == 0 else range(KN, K):
            zz[r, pl.ds(k * rank, rank)] = mm(clt[k], weights, (1, 1)).astype(BF16)
        send_z(part, part)
    for part in range(2):
        send_z(1 - part, part)

    @pl.when(is_mid)
    def _():
        B = "mid"
        far = C - 1 - edge
        relay_other(1)
        arrive(part_of(far, 0), cr_in.at[far, 0])
        send_crt(B, far, 0, edge)

    def relay_z(part, branch):
        via, to = (0, 1) if part == 0 else (1, 0)
        arrive(zpart(across[via], part), z_in.at[via, part])
        send(branch, zpart(across[via], part), zpart(across[via], part), z_in.at[2, part],
             (across[to], c, d), (KN if part == 0 else KM) * SQ)

    part_l = lo_h.shape[1] // D
    place = c * D + d
    owner, slot_l = place // C, lax.rem(place, C)

    def halves(left, right, contract, parts, got, sem, in_s, indices):
        size = left.shape[0] // D

        def keep(n, rows):
            for q, index in enumerate(indices):
                parts[n, index] = rows[:, q * rank:(q + 1) * rank]

        def share(n):
            for index in indices:
                send(sem[0], parts.at[n, index], got.at[index, d], in_s, (r, c, n), 0, sem[1])

        if D == 2:
            for n in (1 - d, d):
                keep(n, mm(left[pl.ds(pl.multiple_of(n * size, size), size), :], right, contract))
                if n is not d:
                    share(n)
        else:
            total = mm(left[...], right, contract)
            for n in range(D):
                keep(n, total[n * size:(n + 1) * size])
            for e in range(1, D):
                share(lax.rem(d + e, D))

    def range_mm(js, indices):
        right = jnp.concatenate([crt[j] for j in js], axis=0)
        halves(lo, right, (1, 1), rps, rpr, ("rp", 4), rp_in.at[indices[0] // 2], indices)

    def range_out(j, index, first, branch="all"):
        total = rps[d, index]
        if index % 2 == 0:
            arrive(rpr.at[pl.ds(index, 2), pl.ds(0, D - 1)], rp_in.at[index // 2])
        for e in range(1, D):
            total = total + rpr[index, lax.rem(d + e, D)]
        rsend[index] = total.astype(BF16)
        if first:
            @pl.when(owner != d)
            def _():
                send("ro", rsend.at[index], rout.at[slot_l], ro_in.at[0], (r, j, owner), part_l * rank * 2, 1)
        else:
            send(branch, rsend.at[index], rout.at[slot_l], ro_in.at[0], (r, j, owner), part_l * rank * 2)

    part_r = ro_h.shape[1] // D
    place_q = r * D + d
    owner_q, slot_q = place_q // R, lax.rem(place_q, R)

    def corange_mm(rows, indices):
        right = jnp.concatenate([zz[i] for i in rows], axis=1)
        halves(ro, right, (1, 0), qps, qpr, ("qp", 5), qp_in.at[(indices[0] + 1) // 2], indices)

    def corange_out(i, index, first):
        total = qps[d, index]
        if index != 2:
            arrive(qpr.at[pl.ds(index, 2 if index == 1 else 1), pl.ds(0, D - 1)], qp_in.at[(index + 1) // 2])
        for e in range(1, D):
            total = total + qpr[index, lax.rem(d + e, D)]
        qsend[index] = total.astype(BF16)
        if first:
            @pl.when(owner_q != d)
            def _():
                send("qo", qsend.at[index], qout.at[slot_q], qo_in.at[0], (i, c, owner_q), part_r * rank * 2, 2)
        else:
            send("all", qsend.at[index], qout.at[slot_q], qo_in.at[0], (i, c, owner_q), part_r * rank * 2)

    order = (c, jnp.where(is_end, near, other), jnp.where(is_end, C - 1 - near, C - 1 - edge),
             jnp.where(is_end, other, edge))

    corange_mm((r,), (0,))

    @pl.when(is_end)
    def _():
        for part in range(2):
            arrive(part_of(near, part), cr_in.at[near, part])

    range_mm(order[:2], (0, 1))

    @pl.when(is_end)
    def _():
        relay_z(0, "end")
        relay_z(1, "end")

    @pl.when(is_mid)
    def _():
        relay_z(0, "mid")
        relay_z(1, "mid")

    for index in range(2):
        range_out(order[index], index, index == 0)

    @pl.when(is_end)
    def _():
        for n in (C - 1 - near, other):
            for part in range(2):
                arrive(part_of(n, part), cr_in.at[n, part])

    @pl.when(is_mid)
    def _():
        for n in (C - 1 - edge, edge):
            arrive(part_of(n, 1), cr_in.at[n, 1])

    range_mm(order[2:], (2, 3))
    arrive(zpart(across[0], 1), z_in.at[0, 1])
    arrive(zpart(across[1], 0), z_in.at[1, 0])
    corange_mm(across[:2], (1, 2))
    range_out(order[2], 2, False)
    range_out(order[3], 3, False)
    corange_out(r, 0, True)
    for slot in range(2):
        corange_out(across[slot], slot + 1, False)
    for part in range(2):
        arrive(zpart(across[2], part), z_in.at[2, part])
    corange_mm(across[2:], (3,))
    corange_out(across[2], 3, False)

    @pl.when(owner == d)
    def _():
        rout[slot_l] = rsend[0]

    @pl.when(owner_q == d)
    def _():
        qout[slot_q] = qsend[0]

    def gather(out, rows, sem, owned):
        count = rows.shape[0]

        @pl.when(owned)
        def _():
            arrive(rows.at[pl.ds(0, count - 1)], sem.at[0])

        @pl.when(jnp.logical_not(owned))
        def _():
            arrive(rows, sem.at[0])

        size = rows.shape[1]
        for q in range(count):
            out[q * size:(q + 1) * size, :] = rows[q]

    gather(out_range, rout, ro_in, owner == d)
    gather(out_corange, qout, qo_in, owner_q == d)
    drain(3, cpr.at[pl.ds(0, D - 1)])
    drain(4, rpr.at[:, pl.ds(0, D - 1)])
    drain(5, qpr.at[:, pl.ds(0, D - 1)])
    for branch, cond in (("mid", is_mid), ("end", is_end)):
        @pl.when(cond)
        def _(branch=branch):
            drain(0, bytes_of(sent["all"] + sent[branch]))
    for branch, cond, sem in (("ro", owner != d, 1), ("qo", owner_q != d, 2)):
        @pl.when(cond)
        def _(branch=branch, sem=sem):
            drain(sem, bytes_of(sent[branch]))


def body(sizes, left_outer, left_inner, right_outer, right_inner, range_test, corange_test, product_mask):
    R, C, D = sizes
    K, BL, rank = left_outer.shape[1:]
    BR = right_outer.shape[2]
    sketch = corange_test.shape[2]
    assert R == 4 and C == 4 and K % R == 0 and BL == BR and BL % D == 0 and D > 1
    KM = K // 2
    KN = K - KM
    KQ = KN // 2
    KR = K // R
    dma = pltpu.SemaphoreType.DMA
    vmem = pltpu.VMEM
    scratch = [
        pltpu.SMEM((1, 1, K), jnp.int32),
        vmem((RULER, rank), BF16),
        vmem((BL, K * rank), BF16),
        vmem((BR, K * rank), BF16),
        vmem((K, BR, rank), BF16),
        vmem((BR, rank), BF16),
        vmem((BL, sketch), BF16),
        vmem((C, K, BL, rank), BF16),
        vmem((R, KN - KQ, rank, BR), BF16),
        vmem((R, KM, 2 * rank, BR), BF16),
        vmem((KQ, rank, BR), BF16),
        vmem((KM, rank, BR), BF16),
        vmem((sketch, K * rank), BF16),
        vmem((sketch, K * rank), BF16),
        vmem((sketch, KM * rank), BF16),
        vmem((sketch, KM * rank), BF16),
        vmem((2, sketch, KM * rank), BF16),
        vmem((sketch, KM * rank), F32),
        vmem((R, rank, KR * rank), F32),
        vmem((R - 1, rank, KR * rank), F32),
        vmem((R, rank, KR * rank), BF16),
        vmem((K, rank, rank), BF16),
        vmem((KM, rank, rank), BF16),
        vmem((KM, rank, rank), BF16),
        vmem((rank, sketch), F32),
        vmem((D, rank, sketch), F32),
        vmem((C, rank, K * rank), BF16),
        vmem((K, rank, sketch), BF16),
        vmem((R, K * rank, rank), BF16),
        vmem((D, C, BL // D, rank), F32),
        vmem((C, D, BL // D, rank), F32),
        vmem((C, BL // D, rank), BF16),
        vmem((C, BL // D, rank), BF16),
        vmem((D, R, BR // D, rank), F32),
        vmem((R, D, BR // D, rank), F32),
        vmem((R, BR // D, rank), BF16),
        vmem((R, BR // D, rank), BF16),
        dma((7,)), dma((6,)),
        dma((C, K)), dma((3, KN - KQ)), dma((2, 4, KM)), dma((3, 2)), dma((1,)), dma((C, 2)), dma((3, 2)),
        dma((2,)), dma((1,)), dma((3,)), dma((1,)),
    ]
    whole = pl.BlockSpec(memory_space=pltpu.VMEM)
    out = jax.ShapeDtypeStruct((BL * C // D, rank), BF16)
    range_rows, corange_rows = pl.pallas_call(
        functools.partial(kernel, (R, C, D, K)),
        out_shape=(out, out),
        in_specs=[pl.BlockSpec(memory_space=pltpu.HBM)] * 7,
        out_specs=(whole, whole),
        scratch_shapes=scratch,
        compiler_params=pltpu.CompilerParams(
            collective_id=0, has_side_effects=True, vmem_limit_bytes=36 * 1024 * 1024
        ),
    )(*[
        pltpu.with_memory_space_constraint(x, pltpu.HBM)
        for x in (left_outer[0], left_inner[0], right_outer[0], right_inner[0],
                  range_test[0], corange_test[0], product_mask)
    ])
    return range_rows[None, None].astype(F32), corange_rows[None, None].astype(F32)


def solution(mesh):
    sizes = tuple(mesh.shape[name] for name in ("row", "col", "depth"))
    return jax.shard_map(
        functools.partial(body, sizes),
        mesh=mesh,
        in_specs=(
            P("row", "depth", "col", None),
            P("row", "depth", "col", None),
            P("col", "depth", "row", None),
            P("col", "depth", "row", None),
            P("col", "row", None),
            P("row", "col", None),
            P("row", "col", "depth"),
        ),
        out_specs=(P("row", "col", "depth", None), P("row", "col", "depth", None)),
        check_vma=False,
    )
```
